32 devices in a mesh: dp: 8 (over z, y), expert: 4 (over x, core).
Axes of the slice: x: 2, y: 2, z: 4, core: 2. Of those that a mesh axis runs over, the one named last changes fastest.
Arguments:
- grad_parts: bfloat16 [8, 12, 704, 2048], P('dp', 'expert'), may hold values from -90 to 90
- momentum: float32 [12, 704, 2048], P('expert', 'dp'), may hold values from -6 to 6
Outputs:
- new_momentum: float32 [12, 704, 2048], P('expert', 'dp')
- muon_update: float32 [12, 704, 2048], P('expert', 'dp')
The draws below stay inside these ranges and needn't reach their ends.
All inputs are finite; a program needn't handle non-finite values.
Results may differ from the reference program's by a relative error of at most 0.023.
Values may be sent and summed in bfloat16 or wider, within the bound.
No kernel may reach another device: no remote copies, remote signals or barrier semaphores. Data moves between devices by JAX's collectives and lax.ppermute only.
A program may use at most 128 MiB of HBM per device.

```python
import math
import jax
import jax.numpy as jnp
from jax import lax

R = 704
C = 2048
NS_ITERS = 3
MATS_DEV = 3
MATS = 12
N_DP = 8
N_EXPERT = 4


def draw_grad_parts(key, part):
    key_own, key_row, key_col = jax.random.split(key, 3)
    own_part = jax.random.normal(key_own, (N_DP, MATS, R, C), jnp.float32)
    row_ramp = 1.0 + 2.0 * jnp.arange(R).astype(jnp.float32) / max(R - 1, 1)
    row_scale = 10.0 ** jax.random.uniform(key_row, (1, MATS, R, 1), jnp.float32)
    row_scale = row_scale * row_ramp.reshape(1, 1, R, 1)
    col_scale = 10.0 ** jax.random.uniform(key_col, (1, MATS, 1, C), jnp.float32)
    group_scale = 1.0 + 2.0 * (jnp.arange(MATS) // MATS_DEV).astype(jnp.float32) / max(N_EXPERT - 1, 1)
    grad = 0.05 * jnp.clip(own_part, -6.0, 6.0) * row_scale * col_scale * group_scale.reshape(1, MATS, 1, 1)
    return jnp.clip(grad, -90.0, 90.0).astype(jnp.bfloat16)


def block_scale(own_key, dims, cuts, smallest, high):
    def one(axis_at, parts):
        steps = jax.random.uniform(jax.random.fold_in(jax.random.fold_in(own_key, 6), axis_at), (parts,), jnp.float32, smallest / len(cuts), high / len(cuts))
        return jnp.repeat(jnp.exp(steps), dims[axis_at] // parts).reshape((-1,) + (1,) * (len(dims) - axis_at - 1))

    factor_of = one(*cuts[0])
    for cut in cuts[1:]:
        factor_of = factor_of * one(*cut)
    return factor_of


def centred(rng, shape, scale, limit, cuts=(), dtype=jnp.bfloat16):
    result = scale * jax.random.normal(rng, shape, jnp.float32)
    if cuts:
        result = result * block_scale(rng, shape, cuts, -0.22, 0.18)
    return jnp.clip(result, -limit, limit).astype(dtype)


def setup_inputs(seed: int = 0) -> dict:
    key_list = jax.random.split(jax.random.key(seed), 3)
    grad_parts = draw_grad_parts(jax.random.fold_in(key_list[2], 71), 0)
    momentum = centred(key_list[1], (MATS, R, C), 1.0, 6.0, ((0, 4), (1, 8)), jnp.float32)
    return {"grad_parts": grad_parts, "momentum": momentum}


momentum_decay = 0.95
coef_a = 3.4445
coef_b = -4.775
coef_c = 2.0315

def orthogonalize(direction):
    flat = direction.astype(jnp.float32)
    norm_value = jnp.sqrt(jnp.sum(flat * flat))
    current = (flat / (norm_value + 1e-07)).astype(jnp.bfloat16)
    for step in range(NS_ITERS):
        gram = jnp.dot(current, current.T, preferred_element_type=jnp.float32).astype(jnp.bfloat16)
        square = jnp.dot(gram, gram, preferred_element_type=jnp.float32)
        poly = (coef_b * gram.astype(jnp.float32) + coef_c * square).astype(jnp.bfloat16)
        current = (coef_a * current.astype(jnp.float32) + jnp.dot(poly, current, preferred_element_type=jnp.float32)).astype(jnp.bfloat16)
    return current

def reference(grad_parts, momentum):
    start = jnp.zeros((MATS, R, C), jnp.float32)

    def accumulate(position, acc):
        return acc + grad_parts[position].astype(jnp.float32)
    grad = lax.fori_loop(0, N_DP, accumulate, start)
    mean_sq = jnp.sum(grad * grad) / (MATS * R * C)
    clip = jnp.minimum(1.0, lax.rsqrt(mean_sq + 1e-06))
    scaled = clip * grad
    new_momentum = momentum_decay * momentum + scaled
    direction = (scaled + momentum_decay * new_momentum).astype(jnp.bfloat16)
    ortho = lax.map(orthogonalize, direction)
    muon_update = 0.2 * math.sqrt(max(R, C)) * ortho.astype(jnp.float32)
    return (new_momentum, muon_update)
```

```python
import math

import jax
import jax.numpy as jnp
from jax import lax
from jax.experimental import pallas as pl
from jax.experimental.pallas import tpu as pltpu
from jax.sharding import PartitionSpec as P

NS_ITERS = 3

momentum_decay = 0.95
coef_a = 3.4445
coef_b = -4.775
coef_c = 2.0315

BF16 = jnp.bfloat16
F32 = jnp.float32


def grid_of(ranks):
    log = ranks.bit_length() - 1
    ny = 2 ** (log // 2) if ranks >= 4 and ranks == 2**log else 1
    return ranks // ny, ny


def cycle_ranks(nz, ny):
    out = [z * ny for z in range(nz)]
    for r in range(nz):
        ys = list(range(1, ny))
        out += [(nz - 1 - r) * ny + y for y in (ys[::-1] if r % 2 else ys)]
    return out


def cycle_position(rank, nz, ny):
    z, y = rank // ny, rank % ny
    r = nz - 1 - z
    return jnp.where(y == 0, z, nz + r * (ny - 1) + jnp.where(r % 2 == 0, y - 1, ny - 1 - y))


def cycle_rank(position, nz, ny):
    q, m = position - nz, max(ny - 1, 1)
    r, k = q // m, q % m
    z = jnp.where(position < nz, position, nz - 1 - r)
    y = jnp.where(position < nz, 0, jnp.where(r % 2 == 0, k + 1, ny - 1 - k))
    return z * ny + y


def stream_widths(columns):
    wide = columns * 5 // 16 // 128 * 128
    return (wide, columns // 2 - wide)


def ring_reduce_scatter(partials, axis):
    ranks = lax.axis_size(axis)
    nz, ny = grid_of(ranks)
    cycle = cycle_ranks(nz, ny)
    pos = cycle_position(lax.axis_index(axis), nz, ny)
    mats, rows_whole, columns = partials.shape
    rows = rows_whole // ranks
    hops = list(zip(cycle, cycle[1:] + cycle[:1]))
    perms = {1: hops, -1: [(b, a) for a, b in hops]}
    widths = stream_widths(columns)
    starts, at = [], 0
    for w in widths:
        starts.append({1: at, -1: at + w})
        at += 2 * w

    def piece(g, d, step):
        dest = cycle_rank((pos - d * (1 + step)) % ranks, nz, ny)
        return lax.dynamic_slice(
            partials, (0, dest * rows, starts[g][d]), (mats, rows, widths[g])
        )

    acc = {(g, d): piece(g, d, 0) for g in range(len(widths)) for d in (1, -1)}
    for step in range(1, ranks):
        for g in range(len(widths)):
            got = {d: lax.ppermute(acc[g, d], axis, perms[d]) for d in (1, -1)}
            if g:
                got[1], got[-1], _, _ = lax.optimization_barrier(
                    (got[1], got[-1], acc[g - 1, 1], acc[g - 1, -1])
                )
            for d in (1, -1):
                total = got[d].astype(F32) + piece(g, d, step).astype(F32)
                acc[g, d] = total.astype(BF16) if step < ranks - 1 else total
    return [acc[g, d] for g in range(len(widths)) for d in (1, -1)]


def owner_ranks(mats, ranks):
    if mats == 3 and ranks == 8:
        return ((2, 4, 1), (3, 5, 6))
    stride = max(ranks // mats, 1)
    return tuple(
        tuple((m * stride + parity * (stride // 2)) % ranks for m in range(mats))
        for parity in (0, 1)
    )


def partner(rank, step, ranks, back=False):
    if ranks & (ranks - 1) == 0:
        return rank ^ step
    return (rank + (ranks - step if back else step)) % ranks


def owner_pairs(owners, step, ranks, experts):
    return [
        (partner(o, step, ranks, back=True) * experts + e, o * experts + e)
        for e in range(experts)
        for o in owners[e % 2]
    ]


def newton_schulz_body(count, block, scale, *refs):
    ins, outs = refs[:count], refs[count : 2 * count]
    d, a, q, qs = refs[2 * count :]
    rows = ins[0].shape[0]
    whole = d.shape[0]
    for i in range(count):
        d[i * rows : (i + 1) * rows, :] = ins[i][...]

    @pl.loop(0, whole // block)
    def _(i):
        r = pl.ds(pl.multiple_of(i * block, 16), block)
        a[r, :] = lax.dot_general(
            d[r, :], d[...], (((1,), (1,)), ((), ())), preferred_element_type=F32
        )

    gram = a[...]
    diagonal = lax.broadcasted_iota(jnp.int32, gram.shape, 0) == lax.broadcasted_iota(
        jnp.int32, gram.shape, 1
    )
    norm = jnp.sqrt(jnp.sum(jnp.where(diagonal, gram, 0.0)))
    inv = 1.0 / (norm + 1e-07)
    a[...] = (gram * inv) * inv
    for step in range(NS_ITERS):
        ab = a[...].astype(BF16)
        poly = coef_b * a[...] + coef_c * jnp.dot(ab, ab, preferred_element_type=F32)
        pb = poly.astype(BF16)
        if step == 0:
            q[...] = jnp.where(diagonal, poly + coef_a, poly)
        else:
            q[...] = coef_a * q[...] + jnp.dot(
                pb, q[...].astype(BF16), preferred_element_type=F32
            )
        if step < NS_ITERS - 1:
            t = jnp.dot(pb, ab, preferred_element_type=F32)
            a[...] = (
                (coef_a * coef_a) * a[...]
                + (2 * coef_a) * t
                + jnp.dot(pb, t.astype(BF16), preferred_element_type=F32)
            )
    qs[...] = (q[...] * (inv * scale)).astype(BF16)
    for i in range(count):
        outs[i][...] = jnp.dot(
            qs[i * rows : (i + 1) * rows, :], d[...], preferred_element_type=F32
        ).astype(BF16)


def newton_schulz(pieces, scale):
    count = len(pieces)
    rows, columns = pieces[0].shape
    whole = count * rows
    block = whole // 2 if whole % 32 == 0 else whole
    vmem = pl.BlockSpec(memory_space=pltpu.VMEM)
    return pl.pallas_call(
        lambda *refs: newton_schulz_body(count, block, scale, *refs),
        out_shape=[jax.ShapeDtypeStruct((rows, columns), BF16)] * count,
        in_specs=[vmem] * count,
        out_specs=[vmem] * count,
        scratch_shapes=[
            pltpu.VMEM((whole, columns), BF16),
            pltpu.VMEM((whole, whole), F32),
            pltpu.VMEM((whole, whole), F32),
            pltpu.VMEM((whole, whole), BF16),
        ],
        compiler_params=pltpu.CompilerParams(vmem_limit_bytes=50 * 2**20),
        name="newton_schulz",
        cost_estimate=pl.CostEstimate(
            flops=4 * whole * whole * columns + 18 * whole**3,
            bytes_accessed=4 * whole * columns,
            transcendentals=0,
        ),
    )(*pieces)


def local(grad_parts, momentum):
    partials = grad_parts[0]
    mats, rows_whole, columns = partials.shape
    ranks, experts = lax.axis_size("dp"), lax.axis_size("expert")
    rank, parity = lax.axis_index("dp"), lax.axis_index("expert") % 2
    both = ("dp", "expert")

    streams = ring_reduce_scatter(partials, "dp")
    square = sum(jnp.sum(s * s) for s in streams)
    squares = lax.all_to_all(
        jnp.full((ranks * experts, 1, 128), square), both, 0, 0, tiled=True
    )
    total = jnp.sum(squares[:, 0, 0])
    factor = jnp.minimum(1.0, lax.rsqrt(total / (mats * experts * rows_whole * columns) + 1e-06))
    summed = jnp.concatenate(streams, axis=2)
    scaled = factor * summed
    new_momentum = momentum_decay * momentum + scaled
    direction = (scaled + momentum_decay * new_momentum).astype(BF16)

    owners = owner_ranks(mats, ranks)
    owner = [jnp.where(parity == 0, owners[0][m], owners[1][m]) for m in range(mats)]
    far_first = list(range(ranks // 2, ranks)) + list(range(1, ranks // 2))
    pieces = [None] * ranks
    for step in [0] + far_first:
        target = partner(rank, step, ranks)
        which = sum(m * (target == owner[m]).astype(jnp.int32) for m in range(mats))
        mine = lax.dynamic_index_in_dim(direction, which, 0, keepdims=False)
        pieces[step] = (
            lax.ppermute(mine, both, owner_pairs(owners, step, ranks, experts)) if step else mine
        )
    result = newton_schulz(pieces, 0.2 * math.sqrt(max(rows_whole, columns)))
    back = [result[0]] + [None] * (ranks - 1)
    for step in far_first:
        pairs = owner_pairs(owners, step, ranks, experts)
        back[step] = lax.ppermute(result[step], both, [(b, a) for a, b in pairs])
    update = []
    for m in range(mats):
        mine = back[0]
        for step in range(1, ranks):
            mine = jnp.where(partner(rank, step, ranks) == owner[m], back[step], mine)
        update.append(mine.astype(F32))
    return (new_momentum, jnp.stack(update))


def solution(mesh):
    return jax.shard_map(
        local,
        mesh=mesh,
        in_specs=(P("dp", "expert", None, None), P("expert", "dp", None)),
        out_specs=(P("expert", "dp", None), P("expert", "dp", None)),
        check_vma=False,
    )
```

```python
import functools
import math

import jax
import jax.numpy as jnp
from jax import lax
from jax.experimental import pallas as pl
from jax.experimental.pallas import tpu as pltpu
from jax.sharding import PartitionSpec as P

NS_ITERS = 3

momentum_decay = 0.95
coef_a = 3.4445
coef_b = -4.775
coef_c = 2.0315

BF16 = jnp.bfloat16
F32 = jnp.float32


def grid_of(ranks):
    log = ranks.bit_length() - 1
    ny = 2 ** (log // 2) if ranks >= 4 and ranks == 2**log else 1
    return ranks // ny, ny


def cycle_ranks(nz, ny):
    out = [z * ny for z in range(nz)]
    for r in range(nz):
        ys = list(range(1, ny))
        out += [(nz - 1 - r) * ny + y for y in (ys[::-1] if r % 2 else ys)]
    return out


def cycle_position(rank, nz, ny):
    z, y = rank // ny, rank % ny
    r = nz - 1 - z
    return jnp.where(y == 0, z, nz + r * (ny - 1) + jnp.where(r % 2 == 0, y - 1, ny - 1 - y))


def cycle_rank(position, nz, ny):
    q, m = position - nz, max(ny - 1, 1)
    r, k = q // m, q % m
    z = jnp.where(position < nz, position, nz - 1 - r)
    y = jnp.where(position < nz, 0, jnp.where(r % 2 == 0, k + 1, ny - 1 - k))
    return z * ny + y


def stream_widths(columns):
    wide = columns * 5 // 16 // 128 * 128
    return (wide, columns // 2 - wide)


def ring_reduce_scatter(partials, axis):
    ranks = lax.axis_size(axis)
    nz, ny = grid_of(ranks)
    cycle = cycle_ranks(nz, ny)
    pos = cycle_position(lax.axis_index(axis), nz, ny)
    mats, rows_whole, columns = partials.shape
    rows = rows_whole // ranks
    hops = list(zip(cycle, cycle[1:] + cycle[:1]))
    perms = {1: hops, -1: [(b, a) for a, b in hops]}
    widths = stream_widths(columns)
    starts, at = [], 0
    for w in widths:
        starts.append({1: at, -1: at + w})
        at += 2 * w

    def piece(g, d, step):
        dest = cycle_rank((pos - d * (1 + step)) % ranks, nz, ny)
        return lax.dynamic_slice(
            partials, (0, dest * rows, starts[g][d]), (mats, rows, widths[g])
        )

    acc = {(g, d): piece(g, d, 0) for g in range(len(widths)) for d in (1, -1)}
    last = {}
    for step in range(1, ranks):
        for g in range(len(widths)):
            got = {d: lax.ppermute(acc[g, d], axis, perms[d]) for d in (1, -1)}
            if g and step < ranks - 1:
                got[1], got[-1], _, _ = lax.optimization_barrier(
                    (got[1], got[-1], acc[g - 1, 1], acc[g - 1, -1])
                )
            for d in (1, -1):
                if step < ranks - 1:
                    acc[g, d] = (got[d].astype(F32) + piece(g, d, step).astype(F32)).astype(BF16)
                else:
                    last[g, d] = (got[d], starts[g][d])
    return [[last[g, d] for d in (1, -1)] for g in range(len(widths))]


VMEM = pl.BlockSpec(memory_space=pltpu.VMEM)
HBM = pl.BlockSpec(memory_space=pltpu.HBM)
SMALL = pltpu.CompilerParams(vmem_limit_bytes=12 * 2**20)


def in_hbm(x):
    return pltpu.with_memory_space_constraint(x, pltpu.HBM)


def lane_sums(x):
    x = jnp.sum(x, axis=0)
    return sum(x[:, c : c + 128] for c in range(0, x.shape[1], 128))


def add_and_square(arrived, own, before, copies, later=()):
    count, fetch = len(arrived), isinstance(own, tuple)
    mats, rows, _ = arrived[0].shape
    partials, axis, columns = own if fetch else (None, None, ())
    shapes = [x.shape for x in arrived] + [shape for shape, _ in later]
    columns = list(columns) + [c for _, c in later]

    def body(*refs):
        refs = list(refs)
        take = lambda n: [refs.pop(0) for _ in range(n)]
        got, (whole,) = take(count), take(1) if fetch else (None,)
        addends = [] if fetch else take(count)
        start = take(1) if before is not None else None
        outs, (squares_out,), extra = take(count), take(1), take(len(later))
        loads = []
        if fetch:
            addends, sems = take(count), refs.pop(0)
            first = pl.multiple_of(lax.axis_index(axis) * rows, 8)
            for i, (ref, c) in enumerate(zip(addends + extra, columns)):
                source = whole.at[:, pl.ds(first, rows), c : c + ref.shape[2]]
                loads.append(pltpu.make_async_copy(source, ref, sems.at[i]))
                loads[-1].start()
        squares = start[0][...] if start else jnp.zeros((rows, 128), F32)
        for i in range(count):
            if fetch:
                loads[i].wait()
            x = got[i][...].astype(F32) + addends[i][...].astype(F32)
            outs[i][...] = x
            squares = squares + lane_sums(x * x)
        for load in loads[count:]:
            load.wait()
        if copies:
            squares = jnp.broadcast_to(jnp.sum(squares), squares_out.shape)
        squares_out[...] = squares

    shape = (copies, 1, 128) if copies else (rows, 128)
    operands = list(arrived) + ([in_hbm(partials)] if fetch else list(own))
    specs = [VMEM] * count + ([HBM] if fetch else [VMEM] * count)
    if before is not None:
        operands, specs = operands + [before], specs + [VMEM]
    outs = pl.pallas_call(
        body,
        out_shape=[jax.ShapeDtypeStruct(x.shape, F32) for x in arrived]
        + [jax.ShapeDtypeStruct(shape, F32)]
        + [jax.ShapeDtypeStruct(shape, BF16) for shape, _ in later],
        in_specs=specs,
        out_specs=[VMEM] * (count + 1 + len(later)),
        scratch_shapes=[pltpu.VMEM(x.shape, BF16) for x in arrived]
        + [pltpu.SemaphoreType.DMA((len(shapes),))]
        if fetch
        else [],
        compiler_params=SMALL,
        name="add_and_square",
    )(*operands)
    return outs[:count], outs[count], list(outs[count + 1 :])


def finish_sums(groups, partials, axis, copies):
    rows = groups[0][0][0].shape[1]
    streams, squares = [], None
    if rows % 8 == 0:
        first, second = [[x for x, _ in g] for g in groups], [[c for _, c in g] for g in groups]
        later = [(x.shape, c) for x, c in groups[1]]
        head, squares, own = add_and_square(
            first[0], (partials, axis, second[0]), None, 0, later
        )
        tail, squares, _ = add_and_square(first[1], own, squares, copies)
        return list(head) + list(tail), squares
    for g, group in enumerate(groups):
        own = [
            lax.dynamic_slice(partials, (0, lax.axis_index(axis) * rows, c), x.shape)
            for x, c in group
        ]
        last = copies if g == len(groups) - 1 else 0
        summed, squares, _ = add_and_square([x for x, _ in group], own, squares, last)
        streams += summed
    return streams, squares


def clip_factor(squares_ref, entries):
    total = jnp.sum(squares_ref[...], axis=0)
    return jnp.minimum(1.0, lax.rsqrt(total / entries + 1e-06))


def column_tiles(streams):
    at = 0
    for i, s in enumerate(streams):
        for c in range(0, s.shape[-1], 128):
            yield i, slice(c, c + 128), slice(at + c, at + c + 128)
        at += s.shape[-1]


def load_rows(source, target, sems):
    loads = [
        pltpu.make_async_copy(source.at[m], target.at[m], sems.at[m]) for m in range(target.shape[0])
    ]
    for load in loads:
        load.start()
    return loads


def my_owners(owners, axes):
    odd = lax.axis_index(axes[1]) % 2 == 1
    return lax.axis_index(axes[0]), [jnp.where(odd, b, a) for a, b in zip(*owners)]


def direction_pieces(squares, streams, momentum, order, owners, axes, entries):
    mats, rows, columns = momentum.shape
    ranks = rounds = len(order)
    count = len(streams)

    def body(squares_ref, *refs):
        ins, whole, outs = refs[:count], refs[count], refs[count + 1 : -2]
        mom, sems = refs[-2:]
        loads = load_rows(whole, mom, sems)
        factor = jnp.broadcast_to(clip_factor(squares_ref, entries), (rows, 128))
        for load in loads:
            load.wait()
        rank, owner = my_owners(owners, axes)
        for step in range(rounds):
            target = partner(rank, order[step], ranks)
            m = functools.reduce(lambda a, b: jnp.where(owner[b] == target, b, a), range(mats), -1)

            @pl.when(m >= 0)
            def _(m=m, step=step):
                for i, here, there in column_tiles(streams):
                    scaled = factor * ins[i][m, :, here]
                    new = momentum_decay * mom[m, :, there] + scaled
                    outs[step][:, there] = (scaled + momentum_decay * new).astype(BF16)

    return pl.pallas_call(
        body,
        out_shape=[jax.ShapeDtypeStruct((rows, columns), BF16)] * rounds,
        in_specs=[VMEM] * (count + 1) + [HBM],
        out_specs=[VMEM] * rounds,
        scratch_shapes=[pltpu.VMEM(momentum.shape, F32), pltpu.SemaphoreType.DMA((mats,))],
        compiler_params=SMALL,
        name="direction_pieces",
    )(squares, *streams, in_hbm(momentum))


def momentum_step(squares, streams, momentum, entries):
    count = len(streams)
    mats, rows, _ = momentum.shape

    def body(squares_ref, *refs):
        ins, whole, out, mom, sems = refs[:count], *refs[count:]
        loads = load_rows(whole, mom, sems)
        factor = jnp.broadcast_to(clip_factor(squares_ref, entries), (rows, 128))
        for m in range(mats):
            loads[m].wait()
            for i, here, there in column_tiles(streams):
                out[m, :, there] = momentum_decay * mom[m, :, there] + factor * ins[i][m, :, here]

    return pl.pallas_call(
        body,
        out_shape=jax.ShapeDtypeStruct(momentum.shape, F32),
        in_specs=[VMEM] * (count + 1) + [HBM],
        out_specs=VMEM,
        scratch_shapes=[pltpu.VMEM(momentum.shape, F32), pltpu.SemaphoreType.DMA((mats,))],
        compiler_params=SMALL,
        name="momentum_step",
    )(squares, *streams, in_hbm(momentum))


def pick_rows(arrived, order, owners, axes):
    rows, columns = arrived[0].shape
    mats, ranks = len(owners[0]), len(order)

    def body(*refs):
        out = refs[-1]
        rank, owner = my_owners(owners, axes)
        for m in range(mats):
            for at, step in enumerate(order):

                @pl.when(partner(owner[m], step, ranks, back=True) == rank)
                def _(m=m, at=at):
                    out[m] = refs[at][...].astype(F32)

    return pl.pallas_call(
        body,
        out_shape=jax.ShapeDtypeStruct((mats, rows, columns), F32),
        in_specs=[VMEM] * len(arrived),
        out_specs=VMEM,
        compiler_params=SMALL,
        name="pick_rows",
    )(*arrived)


def owner_ranks(mats, ranks):
    if mats == 3 and ranks == 8:
        return ((2, 4, 1), (3, 5, 6))
    stride = max(ranks // mats, 1)
    return tuple(
        tuple((m * stride + parity * (stride // 2)) % ranks for m in range(mats))
        for parity in (0, 1)
    )


def partner(rank, step, ranks, back=False):
    if ranks & (ranks - 1) == 0:
        return rank ^ step
    return (rank + (ranks - step if back else step)) % ranks


def owner_pairs(owners, step, ranks, experts):
    return [
        (partner(o, step, ranks, back=True) * experts + e, o * experts + e)
        for e in range(experts)
        for o in owners[e % 2]
    ]


def rounds_of(ranks, back):
    if ranks != 8:
        return list(range(ranks)), {}
    return ([0, 1, 4, 5, 6, 7, 2, 3], {2: 1, 3: 4}) if back else ([0, 1, 4, 5, 2, 3, 6, 7], {6: 1, 7: 2})


def exchange(pieces, axes, owners, ranks, experts, back):
    order, after = rounds_of(ranks, back)
    out = {0: pieces[0]}
    for at, step in enumerate(order):
        if step == 0:
            continue
        piece = pieces[at]
        if step in after:
            piece, _ = lax.optimization_barrier((piece, out[after[step]]))
        pairs = owner_pairs(owners, step, ranks, experts)
        if back:
            pairs = [(b, a) for a, b in pairs]
        out[step] = lax.ppermute(piece, axes, pairs)
    return [out[step] for step in order]


def newton_schulz_body(count, place, block, scale, *refs):
    ins, outs = refs[:count], refs[count : 2 * count]
    d, a, q, qs = refs[2 * count :]
    rows = ins[0].shape[0]
    whole = d.shape[0]
    for i in range(count):
        d[i * rows : (i + 1) * rows, :] = ins[i][...]

    @pl.loop(0, whole // block)
    def _(i):
        r = pl.ds(pl.multiple_of(i * block, 16), block)
        a[r, :] = lax.dot_general(
            d[r, :], d[...], (((1,), (1,)), ((), ())), preferred_element_type=F32
        )

    gram = a[...]
    diagonal = lax.broadcasted_iota(jnp.int32, gram.shape, 0) == lax.broadcasted_iota(
        jnp.int32, gram.shape, 1
    )
    norm = jnp.sqrt(jnp.sum(jnp.where(diagonal, gram, 0.0)))
    inv = 1.0 / (norm + 1e-07)
    a[...] = (gram * inv) * inv
    for step in range(NS_ITERS):
        ab = a[...].astype(BF16)
        poly = coef_b * a[...] + coef_c * jnp.dot(ab, ab, preferred_element_type=F32)
        pb = poly.astype(BF16)
        if step == 0:
            q[...] = jnp.where(diagonal, poly + coef_a, poly)
        else:
            q[...] = coef_a * q[...] + jnp.dot(
                pb, q[...].astype(BF16), preferred_element_type=F32
            )
        if step < NS_ITERS - 1:
            t = jnp.dot(pb, ab, preferred_element_type=F32)
            a[...] = (
                (coef_a * coef_a) * a[...]
                + (2 * coef_a) * t
                + jnp.dot(pb, t.astype(BF16), preferred_element_type=F32)
            )
    qs[...] = (q[...] * (inv * scale)).astype(BF16)
    for i, j in enumerate(place):
        outs[i][...] = jnp.dot(
            qs[j * rows : (j + 1) * rows, :], d[...], preferred_element_type=F32
        ).astype(BF16)


def newton_schulz(pieces, place, scale):
    count = len(pieces)
    rows, columns = pieces[0].shape
    whole = count * rows
    block = whole // 2 if whole % 32 == 0 else whole
    vmem = pl.BlockSpec(memory_space=pltpu.VMEM)
    return pl.pallas_call(
        lambda *refs: newton_schulz_body(count, place, block, scale, *refs),
        out_shape=[jax.ShapeDtypeStruct((rows, columns), BF16)] * count,
        in_specs=[vmem] * count,
        out_specs=[vmem] * count,
        scratch_shapes=[
            pltpu.VMEM((whole, columns), BF16),
            pltpu.VMEM((whole, whole), F32),
            pltpu.VMEM((whole, whole), F32),
            pltpu.VMEM((whole, whole), BF16),
        ],
        compiler_params=pltpu.CompilerParams(vmem_limit_bytes=28 * 2**20),
        name="newton_schulz",
        cost_estimate=pl.CostEstimate(
            flops=4 * whole * whole * columns + 18 * whole**3,
            bytes_accessed=4 * whole * columns,
            transcendentals=0,
        ),
    )(*pieces)


def local(grad_parts, momentum):
    partials = grad_parts[0]
    mats, rows_whole, columns = partials.shape
    ranks, experts = lax.axis_size("dp"), lax.axis_size("expert")
    both = ("dp", "expert")

    groups = ring_reduce_scatter(partials, "dp")
    streams, square = finish_sums(groups, partials, "dp", ranks * experts)
    squares = lax.all_to_all(square, both, 0, 0, tiled=True)
    entries = mats * experts * rows_whole * columns

    owners = owner_ranks(mats, ranks)
    there, _ = rounds_of(ranks, back=False)
    here, _ = rounds_of(ranks, back=True)
    mine = direction_pieces(squares, streams, momentum, there, owners, both, entries)
    new_momentum = momentum_step(squares, streams, momentum, entries)
    pieces = exchange(mine, both, owners, ranks, experts, back=False)
    place = [there.index(step) for step in here]
    result = newton_schulz(pieces, place, 0.2 * math.sqrt(max(rows_whole, columns)))
    arrived = exchange(result, both, owners, ranks, experts, back=True)
    return (new_momentum, pick_rows(arrived, here, owners, both))


def solution(mesh):
    return jax.shard_map(
        local,
        mesh=mesh,
        in_specs=(P("dp", "expert", None, None), P("expert", "dp", None)),
        out_specs=(P("expert", "dp", None), P("expert", "dp", None)),
        check_vma=False,
    )
```

```python
import functools
import math

import jax
import jax.numpy as jnp
from jax import lax
from jax.experimental import pallas as pl
from jax.experimental.pallas import tpu as pltpu
from jax.sharding import PartitionSpec as P

NS_ITERS = 3

momentum_decay = 0.95
coef_a = 3.4445
coef_b = -4.775
coef_c = 2.0315

BF16 = jnp.bfloat16
F32 = jnp.float32


def grid_of(ranks):
    log = ranks.bit_length() - 1
    ny = 2 ** (log // 2) if ranks >= 4 and ranks == 2**log else 1
    return ranks // ny, ny


def cycle_ranks(nz, ny):
    out = [z * ny for z in range(nz)]
    for r in range(nz):
        ys = list(range(1, ny))
        out += [(nz - 1 - r) * ny + y for y in (ys[::-1] if r % 2 else ys)]
    return out


def cycle_position(rank, nz, ny):
    z, y = rank // ny, rank % ny
    r = nz - 1 - z
    return jnp.where(y == 0, z, nz + r * (ny - 1) + jnp.where(r % 2 == 0, y - 1, ny - 1 - y))


def cycle_rank(position, nz, ny):
    q, m = position - nz, max(ny - 1, 1)
    r, k = q // m, q % m
    z = jnp.where(position < nz, position, nz - 1 - r)
    y = jnp.where(position < nz, 0, jnp.where(r % 2 == 0, k + 1, ny - 1 - k))
    return z * ny + y


def stream_widths(columns):
    wide = columns * 5 // 16 // 128 * 128
    return (wide, columns // 2 - wide)


def ring_reduce_scatter(partials, axis):
    ranks = lax.axis_size(axis)
    nz, ny = grid_of(ranks)
    cycle = cycle_ranks(nz, ny)
    pos = cycle_position(lax.axis_index(axis), nz, ny)
    mats, rows_whole, columns = partials.shape
    rows = rows_whole // ranks
    hops = list(zip(cycle, cycle[1:] + cycle[:1]))
    perms = {1: hops, -1: [(b, a) for a, b in hops]}
    widths = stream_widths(columns)
    starts, at = [], 0
    for w in widths:
        starts.append({1: at, -1: at + w})
        at += 2 * w

    def piece(g, d, step):
        dest = cycle_rank((pos - d * (1 + step)) % ranks, nz, ny)
        return lax.dynamic_slice(
            partials, (0, dest * rows, starts[g][d]), (mats, rows, widths[g])
        )

    acc = {(g, d): piece(g, d, 0) for g in range(len(widths)) for d in (1, -1)}
    last = {}
    for step in range(1, ranks):
        for g in range(len(widths)):
            got = {d: lax.ppermute(acc[g, d], axis, perms[d]) for d in (1, -1)}
            if g and step < ranks - 1:
                got[1], got[-1], _, _ = lax.optimization_barrier(
                    (got[1], got[-1], acc[g - 1, 1], acc[g - 1, -1])
                )
            for d in (1, -1):
                if step < ranks - 1:
                    acc[g, d] = (got[d].astype(F32) + piece(g, d, step).astype(F32)).astype(BF16)
                else:
                    last[g, d] = (got[d], starts[g][d])
    return [[last[g, d] for d in (1, -1)] for g in range(len(widths))]


VMEM = pl.BlockSpec(memory_space=pltpu.VMEM)
HBM = pl.BlockSpec(memory_space=pltpu.HBM)
SMALL = pltpu.CompilerParams(vmem_limit_bytes=12 * 2**20)


def in_hbm(x):
    return pltpu.with_memory_space_constraint(x, pltpu.HBM)


def lane_sums(x):
    x = jnp.sum(x, axis=0)
    return sum(x[:, c : c + 128] for c in range(0, x.shape[1], 128))


def add_and_square(arrived, own, before, copies, later=()):
    count, fetch = len(arrived), isinstance(own, tuple)
    mats, rows, _ = arrived[0].shape
    partials, axis, columns = own if fetch else (None, None, ())
    shapes = [x.shape for x in arrived] + [shape for shape, _ in later]
    columns = list(columns) + [c for _, c in later]

    def body(*refs):
        refs = list(refs)
        take = lambda n: [refs.pop(0) for _ in range(n)]
        got, (whole,) = take(count), take(1) if fetch else (None,)
        addends = [] if fetch else take(count)
        start = take(1) if before is not None else None
        outs, (squares_out,), extra = take(count), take(1), take(len(later))
        loads = []
        if fetch:
            addends, sems = take(count), refs.pop(0)
            first = pl.multiple_of(lax.axis_index(axis) * rows, 8)
            for i, (ref, c) in enumerate(zip(addends + extra, columns)):
                source = whole.at[:, pl.ds(first, rows), c : c + ref.shape[2]]
                loads.append(pltpu.make_async_copy(source, ref, sems.at[i]))
                loads[-1].start()
        squares = start[0][...] if start else jnp.zeros((rows, 128), F32)
        for i in range(count):
            if fetch:
                loads[i].wait()
            x = got[i][...].astype(F32) + addends[i][...].astype(F32)
            outs[i][...] = x
            squares = squares + lane_sums(x * x)
        for load in loads[count:]:
            load.wait()
        if copies:
            squares = jnp.broadcast_to(jnp.sum(squares), squares_out.shape)
        squares_out[...] = squares

    shape = (copies, 1, 128) if copies else (rows, 128)
    operands = list(arrived) + ([in_hbm(partials)] if fetch else list(own))
    specs = [VMEM] * count + ([HBM] if fetch else [VMEM] * count)
    if before is not None:
        operands, specs = operands + [before], specs + [VMEM]
    outs = pl.pallas_call(
        body,
        out_shape=[jax.ShapeDtypeStruct(x.shape, F32) for x in arrived]
        + [jax.ShapeDtypeStruct(shape, F32)]
        + [jax.ShapeDtypeStruct(shape, BF16) for shape, _ in later],
        in_specs=specs,
        out_specs=[VMEM] * (count + 1 + len(later)),
        scratch_shapes=[pltpu.VMEM(x.shape, BF16) for x in arrived]
        + [pltpu.SemaphoreType.DMA((len(shapes),))]
        if fetch
        else [],
        compiler_params=SMALL,
        name="add_and_square",
    )(*operands)
    return outs[:count], outs[count], list(outs[count + 1 :])


def finish_sums(groups, partials, axis, copies):
    rows = groups[0][0][0].shape[1]
    streams, squares = [], None
    if rows % 8 == 0:
        first, second = [[x for x, _ in g] for g in groups], [[c for _, c in g] for g in groups]
        later = [(x.shape, c) for x, c in groups[1]]
        head, squares, own = add_and_square(
            first[0], (partials, axis, second[0]), None, 0, later
        )
        tail, squares, _ = add_and_square(first[1], own, squares, copies)
        return list(head) + list(tail), squares
    for g, group in enumerate(groups):
        own = [
            lax.dynamic_slice(partials, (0, lax.axis_index(axis) * rows, c), x.shape)
            for x, c in group
        ]
        last = copies if g == len(groups) - 1 else 0
        summed, squares, _ = add_and_square([x for x, _ in group], own, squares, last)
        streams += summed
    return streams, squares


def clip_factor(squares_ref, entries):
    total = jnp.sum(squares_ref[...], axis=0)
    return jnp.minimum(1.0, lax.rsqrt(total / entries + 1e-06))


def column_tiles(streams):
    at = 0
    for i, s in enumerate(streams):
        for c in range(0, s.shape[-1], 128):
            yield i, slice(c, c + 128), slice(at + c, at + c + 128)
        at += s.shape[-1]


def load_rows(source, target, sems):
    loads = [
        pltpu.make_async_copy(source.at[m], target.at[m], sems.at[m]) for m in range(target.shape[0])
    ]
    for load in loads:
        load.start()
    return loads


def my_owners(owners, axes):
    odd = lax.axis_index(axes[1]) % 2 == 1
    return lax.axis_index(axes[0]), [jnp.where(odd, b, a) for a, b in zip(*owners)]


def direction_pieces(squares, streams, momentum, order, owners, axes, entries):
    mats, rows, columns = momentum.shape
    ranks = rounds = len(order)
    count = len(streams)

    def body(squares_ref, *refs):
        ins, whole, outs = refs[:count], refs[count], refs[count + 1 : -2]
        mom, sems = refs[-2:]
        loads = load_rows(whole, mom, sems)
        factor = jnp.broadcast_to(clip_factor(squares_ref, entries), (rows, 128))
        for load in loads:
            load.wait()
        rank, owner = my_owners(owners, axes)
        for step in range(rounds):
            target = partner(rank, order[step], ranks)
            m = functools.reduce(lambda a, b: jnp.where(owner[b] == target, b, a), range(mats), -1)

            @pl.when(m >= 0)
            def _(m=m, step=step):
                for i, here, there in column_tiles(streams):
                    scaled = factor * ins[i][m, :, here]
                    new = momentum_decay * mom[m, :, there] + scaled
                    outs[step][:, there] = (scaled + momentum_decay * new).astype(BF16)

    return pl.pallas_call(
        body,
        out_shape=[jax.ShapeDtypeStruct((rows, columns), BF16)] * rounds,
        in_specs=[VMEM] * (count + 1) + [HBM],
        out_specs=[VMEM] * rounds,
        scratch_shapes=[pltpu.VMEM(momentum.shape, F32), pltpu.SemaphoreType.DMA((mats,))],
        compiler_params=SMALL,
        name="direction_pieces",
    )(squares, *streams, in_hbm(momentum))


def momentum_step(squares, streams, momentum, entries):
    count = len(streams)
    mats, rows, _ = momentum.shape

    def body(squares_ref, *refs):
        ins, whole, out, mom, sems = refs[:count], *refs[count:]
        loads = load_rows(whole, mom, sems)
        factor = jnp.broadcast_to(clip_factor(squares_ref, entries), (rows, 128))
        for m in range(mats):
            loads[m].wait()
            for i, here, there in column_tiles(streams):
                out[m, :, there] = momentum_decay * mom[m, :, there] + factor * ins[i][m, :, here]

    return pl.pallas_call(
        body,
        out_shape=jax.ShapeDtypeStruct(momentum.shape, F32),
        in_specs=[VMEM] * (count + 1) + [HBM],
        out_specs=VMEM,
        scratch_shapes=[pltpu.VMEM(momentum.shape, F32), pltpu.SemaphoreType.DMA((mats,))],
        compiler_params=SMALL,
        name="momentum_step",
    )(squares, *streams, in_hbm(momentum))


def pick_rows(arrived, order, owners, axes):
    rows, columns = arrived[0].shape
    mats, ranks = len(owners[0]), len(order)

    def body(*refs):
        out = refs[-1]
        rank, owner = my_owners(owners, axes)
        for m in range(mats):
            for at, step in enumerate(order):

                @pl.when(partner(owner[m], step, ranks, back=True) == rank)
                def _(m=m, at=at):
                    out[m] = refs[at][:rows, :].astype(F32)

    return pl.pallas_call(
        body,
        out_shape=jax.ShapeDtypeStruct((mats, rows, columns), F32),
        in_specs=[VMEM] * len(arrived),
        out_specs=VMEM,
        compiler_params=SMALL,
        name="pick_rows",
    )(*arrived)


def owner_ranks(mats, ranks):
    if mats == 3 and ranks == 8:
        return ((2, 4, 1), (3, 5, 6))
    stride = max(ranks // mats, 1)
    return tuple(
        tuple((m * stride + parity * (stride // 2)) % ranks for m in range(mats))
        for parity in (0, 1)
    )


def relayed(mats, ranks):
    return ((1, 4), (3, 6)) if mats == 3 and ranks == 8 else ((), ())


def partner(rank, step, ranks, back=False):
    if ranks & (ranks - 1) == 0:
        return rank ^ step
    return (rank + (ranks - step if back else step)) % ranks


def owner_pairs(owners, step, ranks, experts):
    return [
        (partner(o, step, ranks, back=True) * experts + e, o * experts + e)
        for e in range(experts)
        for o in owners[e % 2]
    ]


def rounds_of(ranks, back):
    if ranks != 8:
        return list(range(ranks)), {}
    return ([0, 1, 4, 5, 6, 7, 2, 3], {2: (1,), 3: (1,)}) if back else ([0, 1, 4, 5, 6, 7, 2, 3], {6: (1,), 7: (1,)})


def exchange(pieces, axes, owners, ranks, experts, relays=None):
    back = relays is not None
    order, after = rounds_of(ranks, back)
    by_way = back and any(relays)
    out = {0: pieces[0]}
    for at, step in enumerate(order):
        if step == 0:
            continue
        piece = pieces[at]
        pairs = owner_pairs(owners, step, ranks, experts)
        if back:
            pairs = [(b, a) for a, b in pairs]
        if by_way and step == ranks - 1:
            hops = {o * experts + e: (o ^ 1) * experts + e for e in range(experts) for o in relays[e % 2]}
            pairs = [(hops.get(a, a), b) for a, b in pairs]
            piece = relay_rows(out[1], piece, relays, axes)
        if step in after:
            piece, *_ = lax.optimization_barrier((piece, *[out[x] for x in after[step]]))
        out[step] = lax.ppermute(piece, axes, pairs)
    return [out[step] for step in order]


def relay_rows(passing, mine, relays, axes):
    rows = mine.shape[0]

    def body(passing_ref, mine_ref, out_ref):
        rank, odd = lax.axis_index(axes[0]), lax.axis_index(axes[1]) % 2 == 1
        passes = functools.reduce(
            jnp.logical_or,
            [rank == jnp.where(odd, b ^ 1, a ^ 1) for a, b in zip(*relays)],
        )

        @pl.when(passes)
        def _():
            out_ref[...] = passing_ref[rows:, :]

        @pl.when(jnp.logical_not(passes))
        def _():
            out_ref[...] = mine_ref[...]

    return pl.pallas_call(
        body,
        out_shape=jax.ShapeDtypeStruct(mine.shape, mine.dtype),
        in_specs=[VMEM] * 2,
        out_specs=VMEM,
        compiler_params=SMALL,
        name="relay_rows",
    )(passing, mine)


def newton_schulz_body(count, place, scale, *refs):
    ins, outs = refs[:count], refs[count : 2 * count]
    d, a, q, qs = refs[2 * count :]
    rows = ins[0].shape[0]
    whole, columns = d.shape
    for i in range(count):
        d[i * rows : (i + 1) * rows, :] = ins[i][...]

    a[...] = lax.dot_general(d[...], d[...], (((1,), (1,)), ((), ())), preferred_element_type=F32)
    gram = a[...]
    diagonal = lax.broadcasted_iota(jnp.int32, gram.shape, 0) == lax.broadcasted_iota(
        jnp.int32, gram.shape, 1
    )
    norm = jnp.sqrt(jnp.sum(jnp.where(diagonal, gram, 0.0)))
    inv = 1.0 / (norm + 1e-07)
    a[...] = (gram * inv) * inv
    for step in range(NS_ITERS):
        ab = a[...].astype(BF16)
        poly = coef_b * a[...] + coef_c * jnp.dot(ab, ab, preferred_element_type=F32)
        pb = poly.astype(BF16)
        if step == 0:
            q[...] = jnp.where(diagonal, poly + coef_a, poly)
        else:
            q[...] = coef_a * q[...] + jnp.dot(
                pb, q[...].astype(BF16), preferred_element_type=F32
            )
        if step < NS_ITERS - 1:
            t = jnp.dot(pb, ab, preferred_element_type=F32)
            a[...] = (
                (coef_a * coef_a) * a[...]
                + (2 * coef_a) * t
                + jnp.dot(pb, t.astype(BF16), preferred_element_type=F32)
            )
    qs[...] = (q[...] * (inv * scale)).astype(BF16)
    width = next(w for w in (512, 256, 128, columns) if columns % w == 0)
    for c in range(0, columns, width):
        x = jnp.dot(qs[...], d[:, c : c + width], preferred_element_type=F32)
        for out, parts in zip(outs, place):
            for i, j in enumerate(parts):
                out[i * rows : (i + 1) * rows, c : c + width] = x[
                    j * rows : (j + 1) * rows, :
                ].astype(BF16)


def newton_schulz(pieces, place, scale):
    count = len(pieces)
    rows, columns = pieces[0].shape
    whole = count * rows
    vmem = pl.BlockSpec(memory_space=pltpu.VMEM)
    return pl.pallas_call(
        lambda *refs: newton_schulz_body(count, place, scale, *refs),
        out_shape=[jax.ShapeDtypeStruct((len(p) * rows, columns), BF16) for p in place],
        in_specs=[vmem] * count,
        out_specs=[vmem] * count,
        scratch_shapes=[
            pltpu.VMEM((whole, columns), BF16),
            pltpu.VMEM((whole, whole), F32),
            pltpu.VMEM((whole, whole), F32),
            pltpu.VMEM((whole, whole), BF16),
        ],
        compiler_params=pltpu.CompilerParams(vmem_limit_bytes=28 * 2**20),
        name="newton_schulz",
        cost_estimate=pl.CostEstimate(
            flops=4 * whole * whole * columns + 18 * whole**3,
            bytes_accessed=4 * whole * columns,
            transcendentals=0,
        ),
    )(*pieces)


def local(grad_parts, momentum):
    partials = grad_parts[0]
    mats, rows_whole, columns = partials.shape
    ranks, experts = lax.axis_size("dp"), lax.axis_size("expert")
    both = ("dp", "expert")

    groups = ring_reduce_scatter(partials, "dp")
    streams, square = finish_sums(groups, partials, "dp", ranks * experts)
    squares = lax.all_to_all(square, both, 0, 0, tiled=True)
    entries = mats * experts * rows_whole * columns

    owners = owner_ranks(mats, ranks)
    there, _ = rounds_of(ranks, back=False)
    here, _ = rounds_of(ranks, back=True)
    mine = direction_pieces(squares, streams, momentum, there, owners, both, entries)
    new_momentum = momentum_step(squares, streams, momentum, entries)
    pieces = exchange(mine, both, owners, ranks, experts)
    relays = relayed(mats, ranks)
    place = [[there.index(step)] for step in here]
    if any(relays):
        place[here.index(1)] += place[here.index(ranks - 1)]
    result = newton_schulz(pieces, place, 0.2 * math.sqrt(max(rows_whole, columns)))
    arrived = exchange(result, both, owners, ranks, experts, relays)
    return (new_momentum, pick_rows(arrived, here, owners, both))


def solution(mesh):
    return jax.shard_map(
        local,
        mesh=mesh,
        in_specs=(P("dp", "expert", None, None), P("expert", "dp", None)),
        out_specs=(P("expert", "dp", None), P("expert", "dp", None)),
        check_vma=False,
    )
```

```python
import functools
import math

import jax
import jax.numpy as jnp
from jax import lax
from jax.experimental import pallas as pl
from jax.experimental.pallas import tpu as pltpu
from jax.sharding import PartitionSpec as P

NS_ITERS = 3

momentum_decay = 0.95
coef_a = 3.4445
coef_b = -4.775
coef_c = 2.0315

BF16 = jnp.bfloat16
F32 = jnp.float32


def grid_of(ranks):
    log = ranks.bit_length() - 1
    ny = 2 ** (log // 2) if ranks >= 4 and ranks == 2**log else 1
    return ranks // ny, ny


def cycle_ranks(nz, ny):
    out = [z * ny for z in range(nz)]
    for r in range(nz):
        ys = list(range(1, ny))
        out += [(nz - 1 - r) * ny + y for y in (ys[::-1] if r % 2 else ys)]
    return out


def cycle_position(rank, nz, ny):
    z, y = rank // ny, rank % ny
    r = nz - 1 - z
    return jnp.where(y == 0, z, nz + r * (ny - 1) + jnp.where(r % 2 == 0, y - 1, ny - 1 - y))


def cycle_rank(position, nz, ny):
    q, m = position - nz, max(ny - 1, 1)
    r, k = q // m, q % m
    z = jnp.where(position < nz, position, nz - 1 - r)
    y = jnp.where(position < nz, 0, jnp.where(r % 2 == 0, k + 1, ny - 1 - k))
    return z * ny + y


def stream_widths(columns):
    wide = columns * 5 // 16 // 128 * 128
    return (wide, columns // 2 - wide)


def ring_reduce_scatter(partials, axis):
    ranks = lax.axis_size(axis)
    nz, ny = grid_of(ranks)
    cycle = cycle_ranks(nz, ny)
    pos = cycle_position(lax.axis_index(axis), nz, ny)
    mats, rows_whole, columns = partials.shape
    rows = rows_whole // ranks
    hops = list(zip(cycle, cycle[1:] + cycle[:1]))
    perms = {1: hops, -1: [(b, a) for a, b in hops]}
    widths = stream_widths(columns)
    starts, at = [], 0
    for w in widths:
        starts.append({1: at, -1: at + w})
        at += 2 * w

    def piece(g, d, step):
        dest = cycle_rank((pos - d * (1 + step)) % ranks, nz, ny)
        return lax.dynamic_slice(
            partials, (0, dest * rows, starts[g][d]), (mats, rows, widths[g])
        )

    acc = {(g, d): piece(g, d, 0) for g in range(len(widths)) for d in (1, -1)}
    last = {}
    for step in range(1, ranks):
        for g in range(len(widths)):
            got = {d: lax.ppermute(acc[g, d], axis, perms[d]) for d in (1, -1)}
            if g and step < ranks - 1:
                got[1], got[-1], _, _ = lax.optimization_barrier(
                    (got[1], got[-1], acc[g - 1, 1], acc[g - 1, -1])
                )
            for d in (1, -1):
                if step < ranks - 1:
                    acc[g, d] = (got[d].astype(F32) + piece(g, d, step).astype(F32)).astype(BF16)
                else:
                    last[g, d] = (got[d], starts[g][d])
    return [[last[g, d] for d in (1, -1)] for g in range(len(widths))]


VMEM = pl.BlockSpec(memory_space=pltpu.VMEM)
HBM = pl.BlockSpec(memory_space=pltpu.HBM)
SMALL = pltpu.CompilerParams(vmem_limit_bytes=12 * 2**20)


def in_hbm(x):
    return pltpu.with_memory_space_constraint(x, pltpu.HBM)


def lane_sums(x):
    x = jnp.sum(x, axis=0)
    return sum(x[:, c : c + 128] for c in range(0, x.shape[1], 128))


def add_and_square(arrived, own, before, copies, later=()):
    count, fetch = len(arrived), isinstance(own, tuple)
    mats, rows, _ = arrived[0].shape
    partials, axis, columns = own if fetch else (None, None, ())
    shapes = [x.shape for x in arrived] + [shape for shape, _ in later]
    columns = list(columns) + [c for _, c in later]

    def body(*refs):
        refs = list(refs)
        take = lambda n: [refs.pop(0) for _ in range(n)]
        got, (whole,) = take(count), take(1) if fetch else (None,)
        addends = [] if fetch else take(count)
        start = take(1) if before is not None else None
        outs, (squares_out,), extra = take(count), take(1), take(len(later))
        loads = []
        if fetch:
            addends, sems = take(count), refs.pop(0)
            first = pl.multiple_of(lax.axis_index(axis) * rows, 8)
            for i, (ref, c) in enumerate(zip(addends + extra, columns)):
                source = whole.at[:, pl.ds(first, rows), c : c + ref.shape[2]]
                loads.append(pltpu.make_async_copy(source, ref, sems.at[i]))
                loads[-1].start()
        squares = start[0][...] if start else jnp.zeros((rows, 128), F32)
        for i in range(count):
            if fetch:
                loads[i].wait()
            x = got[i][...].astype(F32) + addends[i][...].astype(F32)
            outs[i][...] = x
            squares = squares + lane_sums(x * x)
        for load in loads[count:]:
            load.wait()
        if copies:
            squares = jnp.broadcast_to(jnp.sum(squares), squares_out.shape)
        squares_out[...] = squares

    shape = (copies, 1, 128) if copies else (rows, 128)
    operands = list(arrived) + ([in_hbm(partials)] if fetch else list(own))
    specs = [VMEM] * count + ([HBM] if fetch else [VMEM] * count)
    if before is not None:
        operands, specs = operands + [before], specs + [VMEM]
    outs = pl.pallas_call(
        body,
        out_shape=[jax.ShapeDtypeStruct(x.shape, F32) for x in arrived]
        + [jax.ShapeDtypeStruct(shape, F32)]
        + [jax.ShapeDtypeStruct(shape, BF16) for shape, _ in later],
        in_specs=specs,
        out_specs=[VMEM] * (count + 1 + len(later)),
        scratch_shapes=[pltpu.VMEM(x.shape, BF16) for x in arrived]
        + [pltpu.SemaphoreType.DMA((len(shapes),))]
        if fetch
        else [],
        compiler_params=SMALL,
        name="add_and_square",
    )(*operands)
    return outs[:count], outs[count], list(outs[count + 1 :])


def finish_sums(groups, partials, axis, copies):
    rows = groups[0][0][0].shape[1]
    streams, squares = [], None
    if rows % 8 == 0:
        first, second = [[x for x, _ in g] for g in groups], [[c for _, c in g] for g in groups]
        later = [(x.shape, c) for x, c in groups[1]]
        head, squares, own = add_and_square(
            first[0], (partials, axis, second[0]), None, 0, later
        )
        tail, squares, _ = add_and_square(first[1], own, squares, copies)
        return list(head) + list(tail), squares
    for g, group in enumerate(groups):
        own = [
            lax.dynamic_slice(partials, (0, lax.axis_index(axis) * rows, c), x.shape)
            for x, c in group
        ]
        last = copies if g == len(groups) - 1 else 0
        summed, squares, _ = add_and_square([x for x, _ in group], own, squares, last)
        streams += summed
    return streams, squares


def clip_factor(squares_ref, entries):
    total = jnp.sum(squares_ref[...], axis=0)
    return jnp.minimum(1.0, lax.rsqrt(total / entries + 1e-06))


def column_tiles(streams):
    at = 0
    for i, s in enumerate(streams):
        for c in range(0, s.shape[-1], 128):
            yield i, slice(c, c + 128), slice(at + c, at + c + 128)
        at += s.shape[-1]


def load_rows(source, target, sems):
    loads = [
        pltpu.make_async_copy(source.at[m], target.at[m], sems.at[m]) for m in range(target.shape[0])
    ]
    for load in loads:
        load.start()
    return loads


def my_owners(owners, axes):
    odd = lax.axis_index(axes[1]) % 2 == 1
    return lax.axis_index(axes[0]), [jnp.where(odd, b, a) for a, b in zip(*owners)]


def direction_pieces(squares, streams, momentum, order, owners, axes, entries):
    mats, rows, columns = momentum.shape
    ranks = rounds = len(order)
    count = len(streams)

    def body(squares_ref, *refs):
        ins, whole, outs = refs[:count], refs[count], refs[count + 1 : -2]
        mom, sems = refs[-2:]
        loads = load_rows(whole, mom, sems)
        factor = jnp.broadcast_to(clip_factor(squares_ref, entries), (rows, 128))
        for load in loads:
            load.wait()
        rank, owner = my_owners(owners, axes)
        for step in range(rounds):
            target = partner(rank, order[step], ranks)
            m = functools.reduce(lambda a, b: jnp.where(owner[b] == target, b, a), range(mats), -1)

            @pl.when(m >= 0)
            def _(m=m, step=step):
                for i, here, there in column_tiles(streams):
                    scaled = factor * ins[i][m, :, here]
                    new = momentum_decay * mom[m, :, there] + scaled
                    outs[step][:, there] = (scaled + momentum_decay * new).astype(BF16)

    return pl.pallas_call(
        body,
        out_shape=[jax.ShapeDtypeStruct((rows, columns), BF16)] * rounds,
        in_specs=[VMEM] * (count + 1) + [HBM],
        out_specs=[VMEM] * rounds,
        scratch_shapes=[pltpu.VMEM(momentum.shape, F32), pltpu.SemaphoreType.DMA((mats,))],
        compiler_params=SMALL,
        name="direction_pieces",
    )(squares, *streams, in_hbm(momentum))


def momentum_step(squares, streams, momentum, entries):
    count = len(streams)
    mats, rows, _ = momentum.shape

    def body(squares_ref, *refs):
        ins, whole, out, mom, sems = refs[:count], *refs[count:]
        loads = load_rows(whole, mom, sems)
        factor = jnp.broadcast_to(clip_factor(squares_ref, entries), (rows, 128))
        for m in range(mats):
            loads[m].wait()
            for i, here, there in column_tiles(streams):
                out[m, :, there] = momentum_decay * mom[m, :, there] + factor * ins[i][m, :, here]

    return pl.pallas_call(
        body,
        out_shape=jax.ShapeDtypeStruct(momentum.shape, F32),
        in_specs=[VMEM] * (count + 1) + [HBM],
        out_specs=VMEM,
        scratch_shapes=[pltpu.VMEM(momentum.shape, F32), pltpu.SemaphoreType.DMA((mats,))],
        compiler_params=SMALL,
        name="momentum_step",
    )(squares, *streams, in_hbm(momentum))


def pick_rows(arrived, order, owners, axes):
    rows, columns = arrived[0].shape
    mats, ranks = len(owners[0]), len(order)

    def body(*refs):
        out = refs[-1]
        rank, owner = my_owners(owners, axes)
        for m in range(mats):
            for at, step in enumerate(order):

                @pl.when(partner(owner[m], step, ranks, back=True) == rank)
                def _(m=m, at=at):
                    out[m] = refs[at][:rows, :].astype(F32)

    return pl.pallas_call(
        body,
        out_shape=jax.ShapeDtypeStruct((mats, rows, columns), F32),
        in_specs=[VMEM] * len(arrived),
        out_specs=VMEM,
        compiler_params=SMALL,
        name="pick_rows",
    )(*arrived)


def owner_ranks(mats, ranks):
    if mats == 3 and ranks == 8:
        return ((2, 4, 1), (3, 5, 6))
    stride = max(ranks // mats, 1)
    return tuple(
        tuple((m * stride + parity * (stride // 2)) % ranks for m in range(mats))
        for parity in (0, 1)
    )


def relayed(mats, ranks):
    return ((1, 4), (3, 6)) if mats == 3 and ranks == 8 else ((), ())


def partner(rank, step, ranks, back=False):
    if ranks & (ranks - 1) == 0:
        return rank ^ step
    return (rank + (ranks - step if back else step)) % ranks


def owner_pairs(owners, step, ranks, experts):
    return [
        (partner(o, step, ranks, back=True) * experts + e, o * experts + e)
        for e in range(experts)
        for o in owners[e % 2]
    ]


def rounds_of(ranks, back):
    if ranks != 8:
        return list(range(ranks)), {}
    return ([0, 1, 4, 5, 6, 7, 2, 3], {2: (1,), 3: (1,)}) if back else ([0, 1, 4, 5, 6, 7, 2, 3], {6: (1,), 7: (1,)})


def exchange(pieces, axes, owners, ranks, experts, relays=None):
    back = relays is not None
    order, after = rounds_of(ranks, back)
    by_way = back and any(relays)
    out = {0: pieces[0]}
    for at, step in enumerate(order):
        if step == 0:
            continue
        piece = pieces[at]
        pairs = owner_pairs(owners, step, ranks, experts)
        if back:
            pairs = [(b, a) for a, b in pairs]
        if by_way and step == ranks - 1:
            hops = {o * experts + e: (o ^ 1) * experts + e for e in range(experts) for o in relays[e % 2]}
            pairs = [(hops.get(a, a), b) for a, b in pairs]
            piece = relay_rows(out[1], piece, relays, axes)
        if step in after:
            piece, *_ = lax.optimization_barrier((piece, *[out[x] for x in after[step]]))
        out[step] = lax.ppermute(piece, axes, pairs)
    return [out[step] for step in order]


def relay_rows(passing, mine, relays, axes):
    rows = mine.shape[0]

    def body(passing_ref, mine_ref, out_ref):
        rank, odd = lax.axis_index(axes[0]), lax.axis_index(axes[1]) % 2 == 1
        passes = functools.reduce(
            jnp.logical_or,
            [rank == jnp.where(odd, b ^ 1, a ^ 1) for a, b in zip(*relays)],
        )

        @pl.when(passes)
        def _():
            out_ref[...] = passing_ref[rows:, :]

        @pl.when(jnp.logical_not(passes))
        def _():
            out_ref[...] = mine_ref[...]

    return pl.pallas_call(
        body,
        out_shape=jax.ShapeDtypeStruct(mine.shape, mine.dtype),
        in_specs=[VMEM] * 2,
        out_specs=VMEM,
        compiler_params=SMALL,
        name="relay_rows",
    )(passing, mine)


def rows_of(order, rows):
    return {step: slice(i * rows, (i + 1) * rows) for i, step in enumerate(order)}


def stage_of(ranks):
    return ([0, 2, 3, 1, 4, 5, 6, 7], 6, 3) if ranks == 8 else (list(range(ranks)), 0, 0)


def gram_width(height):
    return height // 128 * 128


def first_gram(pieces, place, whole):
    rows, columns = pieces[0].shape
    height = len(pieces) * rows
    width = gram_width(height)

    def body(*refs):
        ins, (d, gram) = refs[:-2], refs[-2:]
        for ref, at in zip(ins, place):
            d[at, :] = ref[...]
        gram[...] = gram_product(d[:height, :], d[:width, :])

    return pl.pallas_call(
        body,
        out_shape=[
            jax.ShapeDtypeStruct((whole, columns), BF16),
            jax.ShapeDtypeStruct((height, width), F32),
        ],
        in_specs=[VMEM] * len(pieces),
        out_specs=[VMEM] * 2,
        compiler_params=SMALL,
        name="first_gram",
        cost_estimate=pl.CostEstimate(
            flops=2 * height * width * columns, bytes_accessed=0, transcendentals=0
        ),
    )(*pieces)


def gram_product(x, y):
    return lax.dot_general(x, y, (((1,), (1,)), ((), ())), preferred_element_type=F32)


def product_rows(qs, d, outs, base, rows):
    columns = d.shape[1]
    width = next(w for w in (512, 256, 128, columns) if columns % w == 0)
    for c in range(0, columns, width):
        x = jnp.dot(qs, d[:, c : c + width], preferred_element_type=F32)
        for ref, parts in outs:
            for i, part in enumerate(parts):
                at = part.start - base
                ref[i * rows : (i + 1) * rows, c : c + width] = x[at : at + rows, :].astype(BF16)


def newton_schulz(pieces, groups, order, early, late, scale):
    rows, columns = pieces[0].shape
    whole = len(order) * rows
    place = rows_of(order, rows)
    height, split = early * rows, late * rows
    width = gram_width(height)
    head = [g for g in groups if g[0] not in order[:late]]
    tail = [g for g in groups if g[0] in order[:late]]

    def body(*refs):
        refs = list(refs)
        take = lambda n: [refs.pop(0) for _ in range(n)]
        _, gram = take(2) if early else (None, None)
        ins, (d, qs), outs = take(len(order) - early), take(2), take(len(head))
        a, q = refs
        for step, ref in zip(order[early:], ins):
            d[place[step], :] = ref[...]
        if early:
            a[:height, :width] = gram[...]
            a[:height, width:] = gram_product(d[:height, :], d[width:, :])
            a[height:, :] = gram_product(d[height:, :], d[...])
        else:
            a[...] = gram_product(d[...], d[...])
        diagonal = lax.broadcasted_iota(jnp.int32, a.shape, 0) == lax.broadcasted_iota(
            jnp.int32, a.shape, 1
        )
        norm = jnp.sqrt(jnp.sum(jnp.where(diagonal, a[...], 0.0)))
        inv = 1.0 / (norm + 1e-07)
        a[...] = (a[...] * inv) * inv
        for step in range(NS_ITERS):
            ab = a[...].astype(BF16)
            poly = coef_b * a[...] + coef_c * jnp.dot(ab, ab, preferred_element_type=F32)
            pb = poly.astype(BF16)
            if step == 0:
                q[...] = jnp.where(diagonal, poly + coef_a, poly)
            else:
                q[...] = coef_a * q[...] + jnp.dot(
                    pb, q[...].astype(BF16), preferred_element_type=F32
                )
            if step < NS_ITERS - 1:
                t = jnp.dot(pb, ab, preferred_element_type=F32)
                a[...] = (
                    (coef_a * coef_a) * a[...]
                    + (2 * coef_a) * t
                    + jnp.dot(pb, t.astype(BF16), preferred_element_type=F32)
                )
        if split:
            qs[...] = (q[:split, :] * (inv * scale)).astype(BF16)
        left = (q[split:, :] * (inv * scale)).astype(BF16)
        parts = [(ref, [place[step] for step in g]) for ref, g in zip(outs, head)]
        product_rows(left, d, parts, split, rows)

    def shapes(lists):
        return [jax.ShapeDtypeStruct((len(g) * rows, columns), BF16) for g in lists]

    soon = [step for step in pieces if step in order[:early]]
    firsts = []
    if early:
        firsts = list(first_gram([pieces[x] for x in soon], [place[x] for x in soon], whole))
    operands = firsts + [pieces[step] for step in order[early:]]
    d, qs, *done = pl.pallas_call(
        body,
        out_shape=[
            jax.ShapeDtypeStruct((whole, columns), BF16),
            jax.ShapeDtypeStruct((split or rows, whole), BF16),
        ]
        + shapes(head),
        in_specs=[VMEM] * len(operands),
        out_specs=[VMEM] * (2 + len(head)),
        scratch_shapes=[pltpu.VMEM((whole, whole), F32), pltpu.VMEM((whole, whole), F32)],
        input_output_aliases={0: 0} if early else {},
        compiler_params=pltpu.CompilerParams(vmem_limit_bytes=28 * 2**20),
        name="newton_schulz",
        cost_estimate=pl.CostEstimate(
            flops=4 * whole * whole * columns + 18 * whole**3,
            bytes_accessed=4 * whole * columns,
            transcendentals=0,
        ),
    )(*operands)
    result = {g[0]: x for g, x in zip(head, done)}
    if tail:

        def last_body(qs_ref, d_ref, *outs):
            parts = [(ref, [place[step] for step in g]) for ref, g in zip(outs, tail)]
            product_rows(qs_ref[...], d_ref, parts, 0, rows)

        done = pl.pallas_call(
            last_body,
            out_shape=shapes(tail),
            in_specs=[VMEM] * 2,
            out_specs=[VMEM] * len(tail),
            compiler_params=SMALL,
            name="last_rows",
            cost_estimate=pl.CostEstimate(
                flops=2 * split * whole * columns, bytes_accessed=0, transcendentals=0
            ),
        )(qs, d)
        result |= {g[0]: x for g, x in zip(tail, done)}
    return [result[g[0]] for g in groups]


def local(grad_parts, momentum):
    partials = grad_parts[0]
    mats, rows_whole, columns = partials.shape
    ranks, experts = lax.axis_size("dp"), lax.axis_size("expert")
    both = ("dp", "expert")

    groups = ring_reduce_scatter(partials, "dp")
    streams, square = finish_sums(groups, partials, "dp", ranks * experts)
    squares = lax.all_to_all(square, both, 0, 0, tiled=True)
    entries = mats * experts * rows_whole * columns

    owners = owner_ranks(mats, ranks)
    there, _ = rounds_of(ranks, back=False)
    here, _ = rounds_of(ranks, back=True)
    mine = direction_pieces(squares, streams, momentum, there, owners, both, entries)
    new_momentum = momentum_step(squares, streams, momentum, entries)
    pieces = exchange(mine, both, owners, ranks, experts)
    relays = relayed(mats, ranks)
    groups = [[step] for step in here]
    if any(relays):
        groups[here.index(1)].append(ranks - 1)
    result = newton_schulz(
        dict(zip(there, pieces)),
        groups,
        *stage_of(ranks),
        0.2 * math.sqrt(max(rows_whole, columns)),
    )
    arrived = exchange(result, both, owners, ranks, experts, relays)
    return (new_momentum, pick_rows(arrived, here, owners, both))


def solution(mesh):
    return jax.shard_map(
        local,
        mesh=mesh,
        in_specs=(P("dp", "expert", None, None), P("expert", "dp", None)),
        out_specs=(P("expert", "dp", None), P("expert", "dp", None)),
        check_vma=False,
    )
```

```python
import functools
import math

import jax
import jax.numpy as jnp
from jax import lax
from jax.experimental import pallas as pl
from jax.experimental.pallas import tpu as pltpu
from jax.sharding import PartitionSpec as P

NS_ITERS = 3

momentum_decay = 0.95
coef_a = 3.4445
coef_b = -4.775
coef_c = 2.0315

BF16 = jnp.bfloat16
F32 = jnp.float32


def grid_of(ranks):
    log = ranks.bit_length() - 1
    ny = 2 ** (log // 2) if ranks >= 4 and ranks == 2**log else 1
    return ranks // ny, ny


def cycle_ranks(nz, ny):
    out = [z * ny for z in range(nz)]
    for r in range(nz):
        ys = list(range(1, ny))
        out += [(nz - 1 - r) * ny + y for y in (ys[::-1] if r % 2 else ys)]
    return out


def cycle_position(rank, nz, ny):
    z, y = rank // ny, rank % ny
    r = nz - 1 - z
    return jnp.where(y == 0, z, nz + r * (ny - 1) + jnp.where(r % 2 == 0, y - 1, ny - 1 - y))


def cycle_rank(position, nz, ny):
    q, m = position - nz, max(ny - 1, 1)
    r, k = q // m, q % m
    z = jnp.where(position < nz, position, nz - 1 - r)
    y = jnp.where(position < nz, 0, jnp.where(r % 2 == 0, k + 1, ny - 1 - k))
    return z * ny + y


def stream_widths(columns):
    wide = columns * 5 // 16 // 128 * 128
    return (wide, columns // 2 - wide)


def ring_reduce_scatter(partials, axis):
    ranks = lax.axis_size(axis)
    nz, ny = grid_of(ranks)
    cycle = cycle_ranks(nz, ny)
    pos = cycle_position(lax.axis_index(axis), nz, ny)
    mats, rows_whole, columns = partials.shape
    rows = rows_whole // ranks
    hops = list(zip(cycle, cycle[1:] + cycle[:1]))
    perms = {1: hops, -1: [(b, a) for a, b in hops]}
    widths = stream_widths(columns)
    starts, at = [], 0
    for w in widths:
        starts.append({1: at, -1: at + w})
        at += 2 * w

    def piece(g, d, step):
        dest = cycle_rank((pos - d * (1 + step)) % ranks, nz, ny)
        return lax.dynamic_slice(
            partials, (0, dest * rows, starts[g][d]), (mats, rows, widths[g])
        )

    acc = {(g, d): piece(g, d, 0) for g in range(len(widths)) for d in (1, -1)}
    last = {}
    for step in range(1, ranks):
        for g in range(len(widths)):
            got = {d: lax.ppermute(acc[g, d], axis, perms[d]) for d in (1, -1)}
            if g and step < ranks - 1:
                got[1], got[-1], _, _ = lax.optimization_barrier(
                    (got[1], got[-1], acc[g - 1, 1], acc[g - 1, -1])
                )
            for d in (1, -1):
                if step < ranks - 1:
                    acc[g, d] = (got[d].astype(F32) + piece(g, d, step).astype(F32)).astype(BF16)
                else:
                    last[g, d] = (got[d], starts[g][d])
    return [[last[g, d] for d in (1, -1)] for g in range(len(widths))]


VMEM = pl.BlockSpec(memory_space=pltpu.VMEM)
HBM = pl.BlockSpec(memory_space=pltpu.HBM)
SMALL = pltpu.CompilerParams(vmem_limit_bytes=12 * 2**20)


def in_hbm(x):
    return pltpu.with_memory_space_constraint(x, pltpu.HBM)


def lane_sums(x):
    x = jnp.sum(x, axis=0)
    return sum(x[:, c : c + 128] for c in range(0, x.shape[1], 128))


def add_and_square(arrived, own, before, copies, later=(), momentum=None):
    count, fetch = len(arrived), isinstance(own, tuple)
    mats, rows, _ = arrived[0].shape
    partials, axis, columns = own if fetch else (None, None, ())
    shapes = [x.shape for x in arrived] + [shape for shape, _ in later]
    columns = list(columns) + [c for _, c in later]

    def body(*refs):
        refs = list(refs)
        take = lambda n: [refs.pop(0) for _ in range(n)]
        got, (whole,) = take(count), take(1) if fetch else (None,)
        addends = [] if fetch else take(count)
        start = take(1) if before is not None else None
        store = take(1) if momentum is not None else None
        outs, (squares_out,), extra = take(count), take(1), take(len(later))
        held = take(1) if momentum is not None else None
        loads = []
        if fetch:
            addends, sems = take(count), refs.pop(0)
            first = pl.multiple_of(lax.axis_index(axis) * rows, 8)
            for i, (ref, c) in enumerate(zip(addends + extra, columns)):
                source = whole.at[:, pl.ds(first, rows), c : c + ref.shape[2]]
                loads.append(pltpu.make_async_copy(source, ref, sems.at[i]))
                loads[-1].start()
            if store:
                loads.append(pltpu.make_async_copy(store[0], held[0], sems.at[len(shapes)]))
                loads[-1].start()
        squares = start[0][...] if start else jnp.zeros((rows, 128), F32)
        for i in range(count):
            if fetch:
                loads[i].wait()
            x = got[i][...].astype(F32) + addends[i][...].astype(F32)
            outs[i][...] = x
            squares = squares + lane_sums(x * x)
        for load in loads[count:]:
            load.wait()
        if copies:
            squares = jnp.broadcast_to(jnp.sum(squares), squares_out.shape)
        squares_out[...] = squares

    shape = (copies, 1, 128) if copies else (rows, 128)
    operands = list(arrived) + ([in_hbm(partials)] if fetch else list(own))
    specs = [VMEM] * count + ([HBM] if fetch else [VMEM] * count)
    if before is not None:
        operands, specs = operands + [before], specs + [VMEM]
    if momentum is not None:
        operands, specs = operands + [in_hbm(momentum)], specs + [HBM]
    held = [] if momentum is None else [jax.ShapeDtypeStruct(momentum.shape, momentum.dtype)]
    outs = pl.pallas_call(
        body,
        out_shape=[jax.ShapeDtypeStruct(x.shape, F32) for x in arrived]
        + [jax.ShapeDtypeStruct(shape, F32)]
        + [jax.ShapeDtypeStruct(shape, BF16) for shape, _ in later]
        + held,
        in_specs=specs,
        out_specs=[VMEM] * (count + 1 + len(later) + len(held)),
        scratch_shapes=[pltpu.VMEM(x.shape, BF16) for x in arrived]
        + [pltpu.SemaphoreType.DMA((len(shapes) + len(held),))]
        if fetch
        else [],
        compiler_params=SMALL,
        name="add_and_square",
    )(*operands)
    return outs[:count], outs[count], list(outs[count + 1 :])


def finish_sums(groups, partials, momentum, axis, copies):
    rows = groups[0][0][0].shape[1]
    streams, squares = [], None
    if rows % 8 == 0:
        first, second = [[x for x, _ in g] for g in groups], [[c for _, c in g] for g in groups]
        later = [(x.shape, c) for x, c in groups[1]]
        head, squares, (*own, momentum) = add_and_square(
            first[0], (partials, axis, second[0]), None, 0, later, momentum
        )
        tail, squares, _ = add_and_square(first[1], own, squares, copies)
        return list(head) + list(tail), squares, momentum
    for g, group in enumerate(groups):
        own = [
            lax.dynamic_slice(partials, (0, lax.axis_index(axis) * rows, c), x.shape)
            for x, c in group
        ]
        last = copies if g == len(groups) - 1 else 0
        summed, squares, _ = add_and_square([x for x, _ in group], own, squares, last)
        streams += summed
    return streams, squares, momentum


def clip_factor(squares_ref, entries):
    total = jnp.sum(squares_ref[...], axis=0)
    return jnp.minimum(1.0, lax.rsqrt(total / entries + 1e-06))


def column_tiles(streams):
    at = 0
    for i, s in enumerate(streams):
        for c in range(0, s.shape[-1], 128):
            yield i, slice(c, c + 128), slice(at + c, at + c + 128)
        at += s.shape[-1]


def my_owners(owners, axes):
    odd = lax.axis_index(axes[1]) % 2 == 1
    return lax.axis_index(axes[0]), [jnp.where(odd, b, a) for a, b in zip(*owners)]


def direction_pieces(squares, streams, momentum, order, owners, axes, entries):
    mats, rows, columns = momentum.shape
    ranks = rounds = len(order)
    count = len(streams)

    def body(squares_ref, *refs):
        ins, mom, outs = refs[:count], refs[count], refs[count + 1 :]
        factor = jnp.broadcast_to(clip_factor(squares_ref, entries), (rows, 128))
        rank, owner = my_owners(owners, axes)
        for step in range(rounds):
            target = partner(rank, order[step], ranks)
            m = functools.reduce(lambda a, b: jnp.where(owner[b] == target, b, a), range(mats), -1)

            @pl.when(m >= 0)
            def _(m=m, step=step):
                for i, here, there in column_tiles(streams):
                    scaled = factor * ins[i][m, :, here]
                    new = momentum_decay * mom[m, :, there] + scaled
                    outs[step][:, there] = (scaled + momentum_decay * new).astype(BF16)

    return pl.pallas_call(
        body,
        out_shape=[jax.ShapeDtypeStruct((rows, columns), BF16)] * rounds,
        in_specs=[VMEM] * (count + 2),
        out_specs=[VMEM] * rounds,
        compiler_params=SMALL,
        name="direction_pieces",
    )(squares, *streams, momentum)


def momentum_step(squares, streams, momentum, entries):
    count = len(streams)
    mats, rows, _ = momentum.shape

    def body(squares_ref, *refs):
        ins, mom, out = refs[:count], refs[count], refs[count + 1]
        factor = jnp.broadcast_to(clip_factor(squares_ref, entries), (rows, 128))
        for m in range(mats):
            for i, here, there in column_tiles(streams):
                out[m, :, there] = momentum_decay * mom[m, :, there] + factor * ins[i][m, :, here]

    return pl.pallas_call(
        body,
        out_shape=jax.ShapeDtypeStruct(momentum.shape, F32),
        in_specs=[VMEM] * (count + 2),
        out_specs=VMEM,
        compiler_params=SMALL,
        name="momentum_step",
    )(squares, *streams, momentum)


def pick_rows(arrived, order, owners, axes):
    rows, columns = arrived[0].shape
    mats, ranks = len(owners[0]), len(order)

    def body(*refs):
        out, wide, sems = refs[ranks:]
        rank, owner = my_owners(owners, axes)
        stores = []
        for m in range(mats):
            for at, step in enumerate(order):

                @pl.when(partner(owner[m], step, ranks, back=True) == rank)
                def _(m=m, at=at):
                    wide[m] = refs[at][:rows, :].astype(F32)

            stores.append(pltpu.make_async_copy(wide.at[m], out.at[m], sems.at[m]))
            stores[m].start()
        for store in stores:
            store.wait()

    return pl.pallas_call(
        body,
        out_shape=jax.ShapeDtypeStruct((mats, rows, columns), F32),
        in_specs=[VMEM] * len(arrived),
        out_specs=HBM,
        scratch_shapes=[pltpu.VMEM((mats, rows, columns), F32), pltpu.SemaphoreType.DMA((mats,))],
        compiler_params=SMALL,
        name="pick_rows",
    )(*arrived)


def owner_ranks(mats, ranks):
    if mats == 3 and ranks == 8:
        return ((2, 4, 1), (3, 5, 6))
    stride = max(ranks // mats, 1)
    return tuple(
        tuple((m * stride + parity * (stride // 2)) % ranks for m in range(mats))
        for parity in (0, 1)
    )


def relayed(mats, ranks):
    return ((1, 4), (3, 6)) if mats == 3 and ranks == 8 else ((), ())


def partner(rank, step, ranks, back=False):
    if ranks & (ranks - 1) == 0:
        return rank ^ step
    return (rank + (ranks - step if back else step)) % ranks


def owner_pairs(owners, step, ranks, experts):
    return [
        (partner(o, step, ranks, back=True) * experts + e, o * experts + e)
        for e in range(experts)
        for o in owners[e % 2]
    ]


def rounds_of(ranks, back):
    if ranks != 8:
        return list(range(ranks)), {}
    return ([0, 1, 4, 5, 6, 7, 2, 3], {2: (1,), 3: (1,)}) if back else ([0, 1, 4, 5, 6, 7, 2, 3], {6: (1,), 7: (1,)})


def exchange(pieces, axes, owners, ranks, experts, relays=None):
    back = relays is not None
    order, after = rounds_of(ranks, back)
    by_way = back and any(relays)
    out = {0: pieces[0]}
    for at, step in enumerate(order):
        if step == 0:
            continue
        piece = pieces[at]
        pairs = owner_pairs(owners, step, ranks, experts)
        if back:
            pairs = [(b, a) for a, b in pairs]
        if by_way and step == ranks - 1:
            hops = {o * experts + e: (o ^ 1) * experts + e for e in range(experts) for o in relays[e % 2]}
            pairs = [(hops.get(a, a), b) for a, b in pairs]
            piece = relay_rows(out[1], piece, relays, axes)
        if step in after:
            piece, *_ = lax.optimization_barrier((piece, *[out[x] for x in after[step]]))
        out[step] = lax.ppermute(piece, axes, pairs)
    return [out[step] for step in order]


def relay_rows(passing, mine, relays, axes):
    rows = mine.shape[0]

    def body(passing_ref, mine_ref, out_ref):
        rank, odd = lax.axis_index(axes[0]), lax.axis_index(axes[1]) % 2 == 1
        passes = functools.reduce(
            jnp.logical_or,
            [rank == jnp.where(odd, b ^ 1, a ^ 1) for a, b in zip(*relays)],
        )

        @pl.when(passes)
        def _():
            out_ref[...] = passing_ref[rows:, :]

        @pl.when(jnp.logical_not(passes))
        def _():
            out_ref[...] = mine_ref[...]

    return pl.pallas_call(
        body,
        out_shape=jax.ShapeDtypeStruct(mine.shape, mine.dtype),
        in_specs=[VMEM] * 2,
        out_specs=VMEM,
        compiler_params=SMALL,
        name="relay_rows",
    )(passing, mine)


def rows_of(order, rows):
    return {step: slice(i * rows, (i + 1) * rows) for i, step in enumerate(order)}


def stage_of(ranks):
    return ([0, 2, 3, 1, 4, 5, 6, 7], 6, 3) if ranks == 8 else (list(range(ranks)), 0, 0)


def gram_width(height):
    return height // 128 * 128


def first_gram(pieces, place, whole):
    rows, columns = pieces[0].shape
    height = len(pieces) * rows
    width = gram_width(height)

    def body(*refs):
        ins, (d, gram) = refs[:-2], refs[-2:]
        for ref, at in zip(ins, place):
            d[at, :] = ref[...]
        gram[...] = gram_product(d[:height, :], d[:width, :])

    return pl.pallas_call(
        body,
        out_shape=[
            jax.ShapeDtypeStruct((whole, columns), BF16),
            jax.ShapeDtypeStruct((height, width), F32),
        ],
        in_specs=[VMEM] * len(pieces),
        out_specs=[VMEM] * 2,
        compiler_params=SMALL,
        name="first_gram",
        cost_estimate=pl.CostEstimate(
            flops=2 * height * width * columns, bytes_accessed=0, transcendentals=0
        ),
    )(*pieces)


def gram_product(x, y):
    return lax.dot_general(x, y, (((1,), (1,)), ((), ())), preferred_element_type=F32)


def product_rows(qs, d, outs, base, rows):
    columns = d.shape[1]
    width = next(w for w in (512, 256, 128, columns) if columns % w == 0)
    for c in range(0, columns, width):
        x = jnp.dot(qs, d[:, c : c + width], preferred_element_type=F32)
        for ref, parts in outs:
            for i, part in enumerate(parts):
                at = part.start - base
                ref[i * rows : (i + 1) * rows, c : c + width] = x[at : at + rows, :].astype(BF16)


def newton_schulz(pieces, groups, order, early, late, scale):
    rows, columns = pieces[0].shape
    whole = len(order) * rows
    place = rows_of(order, rows)
    height, split = early * rows, late * rows
    width = gram_width(height)
    head = [g for g in groups if g[0] not in order[:late]]
    tail = [g for g in groups if g[0] in order[:late]]

    def body(*refs):
        refs = list(refs)
        take = lambda n: [refs.pop(0) for _ in range(n)]
        _, gram = take(2) if early else (None, None)
        ins, (d, qs), outs = take(len(order) - early), take(2), take(len(head))
        a, q = refs
        for step, ref in zip(order[early:], ins):
            d[place[step], :] = ref[...]
        if early:
            a[:height, :width] = gram[...]
            a[:height, width:] = gram_product(d[:height, :], d[width:, :])
            a[height:, :] = gram_product(d[height:, :], d[...])
        else:
            a[...] = gram_product(d[...], d[...])
        diagonal = lax.broadcasted_iota(jnp.int32, a.shape, 0) == lax.broadcasted_iota(
            jnp.int32, a.shape, 1
        )
        norm = jnp.sqrt(jnp.sum(jnp.where(diagonal, a[...], 0.0)))
        inv = 1.0 / (norm + 1e-07)
        a[...] = (a[...] * inv) * inv
        for step in range(NS_ITERS):
            ab = a[...].astype(BF16)
            poly = coef_b * a[...] + coef_c * jnp.dot(ab, ab, preferred_element_type=F32)
            pb = poly.astype(BF16)
            if step == 0:
                q[...] = jnp.where(diagonal, poly + coef_a, poly)
            else:
                q[...] = coef_a * q[...] + jnp.dot(
                    pb, q[...].astype(BF16), preferred_element_type=F32
                )
            if step < NS_ITERS - 1:
                t = jnp.dot(pb, ab, preferred_element_type=F32)
                a[...] = (
                    (coef_a * coef_a) * a[...]
                    + (2 * coef_a) * t
                    + jnp.dot(pb, t.astype(BF16), preferred_element_type=F32)
                )
        if split:
            qs[...] = (q[:split, :] * (inv * scale)).astype(BF16)
        left = (q[split:, :] * (inv * scale)).astype(BF16)
        parts = [(ref, [place[step] for step in g]) for ref, g in zip(outs, head)]
        product_rows(left, d, parts, split, rows)

    def shapes(lists):
        return [jax.ShapeDtypeStruct((len(g) * rows, columns), BF16) for g in lists]

    soon = [step for step in pieces if step in order[:early]]
    firsts = []
    if early:
        firsts = list(first_gram([pieces[x] for x in soon], [place[x] for x in soon], whole))
    operands = firsts + [pieces[step] for step in order[early:]]
    d, qs, *done = pl.pallas_call(
        body,
        out_shape=[
            jax.ShapeDtypeStruct((whole, columns), BF16),
            jax.ShapeDtypeStruct((split or rows, whole), BF16),
        ]
        + shapes(head),
        in_specs=[VMEM] * len(operands),
        out_specs=[VMEM] * (2 + len(head)),
        scratch_shapes=[pltpu.VMEM((whole, whole), F32), pltpu.VMEM((whole, whole), F32)],
        input_output_aliases={0: 0} if early else {},
        compiler_params=pltpu.CompilerParams(vmem_limit_bytes=28 * 2**20),
        name="newton_schulz",
        cost_estimate=pl.CostEstimate(
            flops=4 * whole * whole * columns + 18 * whole**3,
            bytes_accessed=4 * whole * columns,
            transcendentals=0,
        ),
    )(*operands)
    result = {g[0]: x for g, x in zip(head, done)}
    if tail:

        def last_body(qs_ref, d_ref, *outs):
            parts = [(ref, [place[step] for step in g]) for ref, g in zip(outs, tail)]
            product_rows(qs_ref[...], d_ref, parts, 0, rows)

        done = pl.pallas_call(
            last_body,
            out_shape=shapes(tail),
            in_specs=[VMEM] * 2,
            out_specs=[VMEM] * len(tail),
            compiler_params=SMALL,
            name="last_rows",
            cost_estimate=pl.CostEstimate(
                flops=2 * split * whole * columns, bytes_accessed=0, transcendentals=0
            ),
        )(qs, d)
        result |= {g[0]: x for g, x in zip(tail, done)}
    return [result[g[0]] for g in groups]


def local(grad_parts, momentum):
    partials = grad_parts[0]
    mats, rows_whole, columns = partials.shape
    ranks, experts = lax.axis_size("dp"), lax.axis_size("expert")
    both = ("dp", "expert")

    groups = ring_reduce_scatter(partials, "dp")
    streams, square, momentum = finish_sums(groups, partials, momentum, "dp", ranks * experts)
    squares = lax.all_to_all(square, both, 0, 0, tiled=True)
    entries = mats * experts * rows_whole * columns

    owners = owner_ranks(mats, ranks)
    there, _ = rounds_of(ranks, back=False)
    here, _ = rounds_of(ranks, back=True)
    mine = direction_pieces(squares, streams, momentum, there, owners, both, entries)
    new_momentum = momentum_step(squares, streams, momentum, entries)
    pieces = exchange(mine, both, owners, ranks, experts)
    relays = relayed(mats, ranks)
    groups = [[step] for step in here]
    if any(relays):
        groups[here.index(1)].append(ranks - 1)
    result = newton_schulz(
        dict(zip(there, pieces)),
        groups,
        *stage_of(ranks),
        0.2 * math.sqrt(max(rows_whole, columns)),
    )
    arrived = exchange(result, both, owners, ranks, experts, relays)
    return (new_momentum, pick_rows(arrived, here, owners, both))


def solution(mesh):
    return jax.shard_map(
        local,
        mesh=mesh,
        in_specs=(P("dp", "expert", None, None), P("expert", "dp", None)),
        out_specs=(P("expert", "dp", None), P("expert", "dp", None)),
        check_vma=False,
    )
```

```python
import functools
import math

import jax
import jax.numpy as jnp
from jax import lax
from jax.experimental import pallas as pl
from jax.experimental.pallas import tpu as pltpu
from jax.sharding import PartitionSpec as P

NS_ITERS = 3

momentum_decay = 0.95
coef_a = 3.4445
coef_b = -4.775
coef_c = 2.0315

BF16 = jnp.bfloat16
F32 = jnp.float32


def grid_of(ranks):
    log = ranks.bit_length() - 1
    ny = 2 ** (log // 2) if ranks >= 4 and ranks == 2**log else 1
    return ranks // ny, ny


def cycle_ranks(nz, ny):
    out = [z * ny for z in range(nz)]
    for r in range(nz):
        ys = list(range(1, ny))
        out += [(nz - 1 - r) * ny + y for y in (ys[::-1] if r % 2 else ys)]
    return out


def cycle_position(rank, nz, ny):
    z, y = rank // ny, rank % ny
    r = nz - 1 - z
    return jnp.where(y == 0, z, nz + r * (ny - 1) + jnp.where(r % 2 == 0, y - 1, ny - 1 - y))


def cycle_rank(position, nz, ny):
    q, m = position - nz, max(ny - 1, 1)
    r, k = q // m, q % m
    z = jnp.where(position < nz, position, nz - 1 - r)
    y = jnp.where(position < nz, 0, jnp.where(r % 2 == 0, k + 1, ny - 1 - k))
    return z * ny + y


def stream_widths(columns):
    wide = columns * 5 // 16 // 128 * 128
    return (wide, columns // 2 - wide)


def ring_reduce_scatter(partials, axis):
    ranks = lax.axis_size(axis)
    nz, ny = grid_of(ranks)
    cycle = cycle_ranks(nz, ny)
    pos = cycle_position(lax.axis_index(axis), nz, ny)
    mats, rows_whole, columns = partials.shape
    rows = rows_whole // ranks
    hops = list(zip(cycle, cycle[1:] + cycle[:1]))
    perms = {1: hops, -1: [(b, a) for a, b in hops]}
    widths = stream_widths(columns)
    starts, at = [], 0
    for w in widths:
        starts.append({1: at, -1: at + w})
        at += 2 * w

    def piece(g, d, step):
        dest = cycle_rank((pos - d * (1 + step)) % ranks, nz, ny)
        return lax.dynamic_slice(
            partials, (0, dest * rows, starts[g][d]), (mats, rows, widths[g])
        )

    acc = {(g, d): piece(g, d, 0) for g in range(len(widths)) for d in (1, -1)}
    last = {}
    for step in range(1, ranks):
        for g in range(len(widths)):
            got = {d: lax.ppermute(acc[g, d], axis, perms[d]) for d in (1, -1)}
            if g and step < ranks - 1:
                got[1], got[-1], _, _ = lax.optimization_barrier(
                    (got[1], got[-1], acc[g - 1, 1], acc[g - 1, -1])
                )
            for d in (1, -1):
                if step < ranks - 1:
                    acc[g, d] = (got[d].astype(F32) + piece(g, d, step).astype(F32)).astype(BF16)
                else:
                    last[g, d] = (got[d], starts[g][d])
    return [[last[g, d] for d in (1, -1)] for g in range(len(widths))]


VMEM = pl.BlockSpec(memory_space=pltpu.VMEM)
HBM = pl.BlockSpec(memory_space=pltpu.HBM)
SMALL = pltpu.CompilerParams(vmem_limit_bytes=12 * 2**20)


def in_hbm(x):
    return pltpu.with_memory_space_constraint(x, pltpu.HBM)


def lane_sums(x):
    x = jnp.sum(x, axis=0)
    return sum(x[:, c : c + 128] for c in range(0, x.shape[1], 128))


def add_and_square(arrived, own, before, copies, later=(), momentum=None):
    count, fetch = len(arrived), isinstance(own, tuple)
    mats, rows, _ = arrived[0].shape
    partials, axis, columns = own if fetch else (None, None, ())
    shapes = [x.shape for x in arrived] + [shape for shape, _ in later]
    columns = list(columns) + [c for _, c in later]

    def body(*refs):
        refs = list(refs)
        take = lambda n: [refs.pop(0) for _ in range(n)]
        got, (whole,) = take(count), take(1) if fetch else (None,)
        addends = [] if fetch else take(count)
        start = take(1) if before is not None else None
        store = take(1) if momentum is not None else None
        outs, (squares_out,), extra = take(count), take(1), take(len(later))
        held = take(1) if momentum is not None else None
        loads = []
        if fetch:
            addends, sems = take(count), refs.pop(0)
            first = pl.multiple_of(lax.axis_index(axis) * rows, 8)
            for i, (ref, c) in enumerate(zip(addends + extra, columns)):
                source = whole.at[:, pl.ds(first, rows), c : c + ref.shape[2]]
                loads.append(pltpu.make_async_copy(source, ref, sems.at[i]))
                loads[-1].start()
            if store:
                loads.append(pltpu.make_async_copy(store[0], held[0], sems.at[len(shapes)]))
                loads[-1].start()
        squares = start[0][...] if start else jnp.zeros((rows, 128), F32)
        for i in range(count):
            if fetch:
                loads[i].wait()
            x = got[i][...].astype(F32) + addends[i][...].astype(F32)
            outs[i][...] = x
            squares = squares + lane_sums(x * x)
        for load in loads[count:]:
            load.wait()
        if copies:
            squares = jnp.broadcast_to(jnp.sum(squares), squares_out.shape)
        squares_out[...] = squares

    shape = (copies, 1, 128) if copies else (rows, 128)
    operands = list(arrived) + ([in_hbm(partials)] if fetch else list(own))
    specs = [VMEM] * count + ([HBM] if fetch else [VMEM] * count)
    if before is not None:
        operands, specs = operands + [before], specs + [VMEM]
    if momentum is not None:
        operands, specs = operands + [in_hbm(momentum)], specs + [HBM]
    held = [] if momentum is None else [jax.ShapeDtypeStruct(momentum.shape, momentum.dtype)]
    outs = pl.pallas_call(
        body,
        out_shape=[jax.ShapeDtypeStruct(x.shape, F32) for x in arrived]
        + [jax.ShapeDtypeStruct(shape, F32)]
        + [jax.ShapeDtypeStruct(shape, BF16) for shape, _ in later]
        + held,
        in_specs=specs,
        out_specs=[VMEM] * (count + 1 + len(later) + len(held)),
        scratch_shapes=[pltpu.VMEM(x.shape, BF16) for x in arrived]
        + [pltpu.SemaphoreType.DMA((len(shapes) + len(held),))]
        if fetch
        else [],
        compiler_params=SMALL,
        name="add_and_square",
    )(*operands)
    return outs[:count], outs[count], list(outs[count + 1 :])


def finish_sums(groups, partials, momentum, axis, copies):
    rows = groups[0][0][0].shape[1]
    streams, squares = [], None
    if rows % 8 == 0:
        first, second = [[x for x, _ in g] for g in groups], [[c for _, c in g] for g in groups]
        later = [(x.shape, c) for x, c in groups[1]]
        head, squares, (*own, momentum) = add_and_square(
            first[0], (partials, axis, second[0]), None, 0, later, momentum
        )
        tail, squares, _ = add_and_square(first[1], own, squares, copies)
        return list(head) + list(tail), squares, momentum
    for g, group in enumerate(groups):
        own = [
            lax.dynamic_slice(partials, (0, lax.axis_index(axis) * rows, c), x.shape)
            for x, c in group
        ]
        last = copies if g == len(groups) - 1 else 0
        summed, squares, _ = add_and_square([x for x, _ in group], own, squares, last)
        streams += summed
    return streams, squares, momentum


def clip_factor(squares_ref, entries):
    total = jnp.sum(squares_ref[...], axis=0)
    return jnp.minimum(1.0, lax.rsqrt(total / entries + 1e-06))


def column_tiles(streams):
    at = 0
    for i, s in enumerate(streams):
        for c in range(0, s.shape[-1], 128):
            yield i, slice(c, c + 128), slice(at + c, at + c + 128)
        at += s.shape[-1]


def my_owners(owners, axes):
    odd = lax.axis_index(axes[1]) % 2 == 1
    return lax.axis_index(axes[0]), [jnp.where(odd, b, a) for a, b in zip(*owners)]


def direction_pieces(squares, streams, momentum, order, owners, axes, entries):
    mats, rows, columns = momentum.shape
    ranks = rounds = len(order)
    count = len(streams)

    def body(squares_ref, *refs):
        ins, mom, outs = refs[:count], refs[count], refs[count + 1 :]
        factor = jnp.broadcast_to(clip_factor(squares_ref, entries), (rows, 128))
        rank, owner = my_owners(owners, axes)
        for step in range(rounds):
            target = partner(rank, order[step], ranks)
            m = functools.reduce(lambda a, b: jnp.where(owner[b] == target, b, a), range(mats), -1)

            @pl.when(m >= 0)
            def _(m=m, step=step):
                for i, here, there in column_tiles(streams):
                    scaled = factor * ins[i][m, :, here]
                    new = momentum_decay * mom[m, :, there] + scaled
                    outs[step][:, there] = (scaled + momentum_decay * new).astype(BF16)

    return pl.pallas_call(
        body,
        out_shape=[jax.ShapeDtypeStruct((rows, columns), BF16)] * rounds,
        in_specs=[VMEM] * (count + 2),
        out_specs=[VMEM] * rounds,
        compiler_params=SMALL,
        name="direction_pieces",
    )(squares, *streams, momentum)


def momentum_step(squares, streams, momentum, entries):
    count = len(streams)
    mats, rows, _ = momentum.shape

    def body(squares_ref, *refs):
        ins, mom, out = refs[:count], refs[count], refs[count + 1]
        factor = jnp.broadcast_to(clip_factor(squares_ref, entries), (rows, 128))
        for m in range(mats):
            for i, here, there in column_tiles(streams):
                out[m, :, there] = momentum_decay * mom[m, :, there] + factor * ins[i][m, :, here]

    return pl.pallas_call(
        body,
        out_shape=jax.ShapeDtypeStruct(momentum.shape, F32),
        in_specs=[VMEM] * (count + 2),
        out_specs=VMEM,
        compiler_params=SMALL,
        name="momentum_step",
    )(squares, *streams, momentum)


def pick_rows(arrived, order, owners, axes):
    rows, columns = arrived[0].shape
    mats, ranks = len(owners[0]), len(order)

    def body(*refs):
        out, wide, sems = refs[ranks:]
        rank, owner = my_owners(owners, axes)
        stores = []
        for m in range(mats):
            for at, step in enumerate(order):

                @pl.when(partner(owner[m], step, ranks, back=True) == rank)
                def _(m=m, at=at):
                    wide[m] = refs[at][:rows, :].astype(F32)

            stores.append(pltpu.make_async_copy(wide.at[m], out.at[m], sems.at[m]))
            stores[m].start()
        for store in stores:
            store.wait()

    return pl.pallas_call(
        body,
        out_shape=jax.ShapeDtypeStruct((mats, rows, columns), F32),
        in_specs=[VMEM] * len(arrived),
        out_specs=HBM,
        scratch_shapes=[pltpu.VMEM((mats, rows, columns), F32), pltpu.SemaphoreType.DMA((mats,))],
        compiler_params=SMALL,
        name="pick_rows",
    )(*arrived)


def owner_ranks(mats, ranks):
    if mats == 3 and ranks == 8:
        return ((2, 4, 1), (3, 5, 6))
    stride = max(ranks // mats, 1)
    return tuple(
        tuple((m * stride + parity * (stride // 2)) % ranks for m in range(mats))
        for parity in (0, 1)
    )


def relayed(mats, ranks):
    return ((1, 4), (3, 6)) if mats == 3 and ranks == 8 else ((), ())


def partner(rank, step, ranks, back=False):
    if ranks & (ranks - 1) == 0:
        return rank ^ step
    return (rank + (ranks - step if back else step)) % ranks


def owner_pairs(owners, step, ranks, experts):
    return [
        (partner(o, step, ranks, back=True) * experts + e, o * experts + e)
        for e in range(experts)
        for o in owners[e % 2]
    ]


def rounds_of(ranks, back):
    if ranks != 8:
        return list(range(ranks)), {}
    return ([0, 1, 7, 4, 5, 6, 2, 3], {2: (1,), 3: (1,)}) if back else ([0, 1, 4, 5, 6, 7, 2, 3], {6: (1,), 7: (1,)})


def exchange(pieces, axes, owners, ranks, experts, relays=None):
    back = relays is not None
    order, after = rounds_of(ranks, back)
    by_way = back and any(relays)
    passed = []
    out = {0: pieces[0]}
    for at, step in enumerate(order):
        if step == 0:
            continue
        piece = pieces[at]
        pairs = owner_pairs(owners, step, ranks, experts)
        if back:
            pairs = [(b, a) for a, b in pairs]
        if by_way and step == ranks - 1:
            hops = {o * experts + e: (o ^ 1) * experts + e for e in range(experts) for o in relays[e % 2]}
            pairs = [(hops.get(a, a), b) for a, b in pairs]
            piece = relay_rows(out[1], piece, relays, axes)
            passed = [piece]
        if step in after:
            waits = [out[x] for x in after[step]] + passed
            piece, *_ = lax.optimization_barrier((piece, *waits))
        out[step] = lax.ppermute(piece, axes, pairs)
    return [out[step] for step in order]


def relay_rows(passing, mine, relays, axes):
    rows = mine.shape[0]

    def body(passing_ref, mine_ref, out_ref):
        rank, odd = lax.axis_index(axes[0]), lax.axis_index(axes[1]) % 2 == 1
        passes = functools.reduce(
            jnp.logical_or,
            [rank == jnp.where(odd, b ^ 1, a ^ 1) for a, b in zip(*relays)],
        )

        @pl.when(passes)
        def _():
            out_ref[...] = passing_ref[rows:, :]

        @pl.when(jnp.logical_not(passes))
        def _():
            out_ref[...] = mine_ref[...]

    return pl.pallas_call(
        body,
        out_shape=jax.ShapeDtypeStruct(mine.shape, mine.dtype),
        in_specs=[VMEM] * 2,
        out_specs=VMEM,
        compiler_params=SMALL,
        name="relay_rows",
    )(passing, mine)


def rows_of(order, rows):
    return {step: slice(i * rows, (i + 1) * rows) for i, step in enumerate(order)}


def stage_of(ranks):
    return ([0, 2, 3, 1, 4, 5, 6, 7], 6, 3) if ranks == 8 else (list(range(ranks)), 0, 0)


def gram_width(height):
    return height // 128 * 128


def first_gram(pieces, place, whole):
    rows, columns = pieces[0].shape
    height = len(pieces) * rows
    width = gram_width(height)

    def body(*refs):
        ins, (d, gram) = refs[:-2], refs[-2:]
        for ref, at in zip(ins, place):
            d[at, :] = ref[...]
        gram[...] = gram_product(d[:height, :], d[:width, :])

    return pl.pallas_call(
        body,
        out_shape=[
            jax.ShapeDtypeStruct((whole, columns), BF16),
            jax.ShapeDtypeStruct((height, width), F32),
        ],
        in_specs=[VMEM] * len(pieces),
        out_specs=[VMEM] * 2,
        compiler_params=SMALL,
        name="first_gram",
        cost_estimate=pl.CostEstimate(
            flops=2 * height * width * columns, bytes_accessed=0, transcendentals=0
        ),
    )(*pieces)


def gram_product(x, y):
    return lax.dot_general(x, y, (((1,), (1,)), ((), ())), preferred_element_type=F32)


def product_rows(qs, d, outs, base, rows):
    columns = d.shape[1]
    width = next(w for w in (512, 256, 128, columns) if columns % w == 0)
    for c in range(0, columns, width):
        x = jnp.dot(qs, d[:, c : c + width], preferred_element_type=F32)
        for ref, parts in outs:
            for i, part in enumerate(parts):
                at = part.start - base
                ref[i * rows : (i + 1) * rows, c : c + width] = x[at : at + rows, :].astype(BF16)


def newton_schulz(pieces, groups, order, early, late, scale):
    rows, columns = pieces[0].shape
    whole = len(order) * rows
    place = rows_of(order, rows)
    height, split = early * rows, late * rows
    width = gram_width(height)
    head = [g for g in groups if g[0] not in order[:late]]
    tail = [g for g in groups if g[0] in order[:late]]

    def body(*refs):
        refs = list(refs)
        take = lambda n: [refs.pop(0) for _ in range(n)]
        _, gram = take(2) if early else (None, None)
        ins, (d, qs), outs = take(len(order) - early), take(2), take(len(head))
        a, q = refs
        for step, ref in zip(order[early:], ins):
            d[place[step], :] = ref[...]
        if early:
            a[:height, :width] = gram[...]
            a[:height, width:] = gram_product(d[:height, :], d[width:, :])
            a[height:, :] = gram_product(d[height:, :], d[...])
        else:
            a[...] = gram_product(d[...], d[...])
        diagonal = lax.broadcasted_iota(jnp.int32, a.shape, 0) == lax.broadcasted_iota(
            jnp.int32, a.shape, 1
        )
        squares = jnp.zeros((1, 1), F32)
        for c in range(0, whole, 128):
            n = min(128, whole - c)
            block = jnp.where(diagonal[:n, :n], a[c : c + n, c : c + n], 0.0)
            squares = squares + jnp.sum(block, keepdims=True)
        norm = jnp.sqrt(squares)
        inv = 1.0 / (norm + 1e-07)
        a[...] = (a[...] * inv) * inv
        for step in range(NS_ITERS):
            ab = a[...].astype(BF16)
            poly = coef_b * a[...] + coef_c * jnp.dot(ab, ab, preferred_element_type=F32)
            pb = poly.astype(BF16)
            if step == 0:
                q[...] = jnp.where(diagonal, poly + coef_a, poly)
            else:
                q[...] = coef_a * q[...] + jnp.dot(
                    pb, q[...].astype(BF16), preferred_element_type=F32
                )
            if step < NS_ITERS - 1:
                t = jnp.dot(pb, ab, preferred_element_type=F32)
                a[...] = (
                    (coef_a * coef_a) * a[...]
                    + (2 * coef_a) * t
                    + jnp.dot(pb, t.astype(BF16), preferred_element_type=F32)
                )
        if split:
            qs[...] = (q[:split, :] * (inv * scale)).astype(BF16)
        left = (q[split:, :] * (inv * scale)).astype(BF16)
        parts = [(ref, [place[step] for step in g]) for ref, g in zip(outs, head)]
        product_rows(left, d, parts, split, rows)

    def shapes(lists):
        return [jax.ShapeDtypeStruct((len(g) * rows, columns), BF16) for g in lists]

    soon = [step for step in pieces if step in order[:early]]
    firsts = []
    if early:
        firsts = list(first_gram([pieces[x] for x in soon], [place[x] for x in soon], whole))
    operands = firsts + [pieces[step] for step in order[early:]]
    d, qs, *done = pl.pallas_call(
        body,
        out_shape=[
            jax.ShapeDtypeStruct((whole, columns), BF16),
            jax.ShapeDtypeStruct((split or rows, whole), BF16),
        ]
        + shapes(head),
        in_specs=[VMEM] * len(operands),
        out_specs=[VMEM] * (2 + len(head)),
        scratch_shapes=[pltpu.VMEM((whole, whole), F32), pltpu.VMEM((whole, whole), F32)],
        input_output_aliases={0: 0} if early else {},
        compiler_params=pltpu.CompilerParams(vmem_limit_bytes=28 * 2**20),
        name="newton_schulz",
        cost_estimate=pl.CostEstimate(
            flops=4 * whole * whole * columns + 18 * whole**3,
            bytes_accessed=4 * whole * columns,
            transcendentals=0,
        ),
    )(*operands)
    result = {g[0]: x for g, x in zip(head, done)}
    if tail:

        def last_body(qs_ref, d_ref, *outs):
            parts = [(ref, [place[step] for step in g]) for ref, g in zip(outs, tail)]
            product_rows(qs_ref[...], d_ref, parts, 0, rows)

        done = pl.pallas_call(
            last_body,
            out_shape=shapes(tail),
            in_specs=[VMEM] * 2,
            out_specs=[VMEM] * len(tail),
            compiler_params=SMALL,
            name="last_rows",
            cost_estimate=pl.CostEstimate(
                flops=2 * split * whole * columns, bytes_accessed=0, transcendentals=0
            ),
        )(qs, d)
        result |= {g[0]: x for g, x in zip(tail, done)}
    return [result[g[0]] for g in groups]


def local(grad_parts, momentum):
    partials = grad_parts[0]
    mats, rows_whole, columns = partials.shape
    ranks, experts = lax.axis_size("dp"), lax.axis_size("expert")
    both = ("dp", "expert")

    groups = ring_reduce_scatter(partials, "dp")
    streams, square, momentum = finish_sums(groups, partials, momentum, "dp", ranks * experts)
    squares = lax.all_to_all(square, both, 0, 0, tiled=True)
    entries = mats * experts * rows_whole * columns

    owners = owner_ranks(mats, ranks)
    there, _ = rounds_of(ranks, back=False)
    here, _ = rounds_of(ranks, back=True)
    mine = direction_pieces(squares, streams, momentum, there, owners, both, entries)
    new_momentum = momentum_step(squares, streams, momentum, entries)
    pieces = exchange(mine, both, owners, ranks, experts)
    relays = relayed(mats, ranks)
    groups = [[step] for step in here]
    if any(relays):
        groups[here.index(1)].append(ranks - 1)
    result = newton_schulz(
        dict(zip(there, pieces)),
        groups,
        *stage_of(ranks),
        0.2 * math.sqrt(max(rows_whole, columns)),
    )
    arrived = exchange(result, both, owners, ranks, experts, relays)
    return (new_momentum, pick_rows(arrived, here, owners, both))


def solution(mesh):
    return jax.shard_map(
        local,
        mesh=mesh,
        in_specs=(P("dp", "expert", None, None), P("expert", "dp", None)),
        out_specs=(P("expert", "dp", None), P("expert", "dp", None)),
        check_vma=False,
    )
```
